32 devices in a mesh: mode: 8 (over y, x, core), rows: 4 (over z).
Axes of the slice: x: 2, y: 2, z: 4, core: 2. Of those that a mesh axis runs over, the one named last changes fastest.
Arguments:
- tangents: float32 [128, 3, 32, 1024], P('mode', None, 'rows'), may hold values from -6 to 6
- checkpoints: float32 [8, 3, 32, 1024], P(None, None, 'rows', 'mode'), may hold values from 0 to 0.5
- owner_order: int32 [8], replicated, may hold values from 0 to 7, each once
- land_mask: int32 [32, 1024], P('rows'), may hold values 0 or 1
- coefficients: float32 [128, 128], replicated, may hold values from -0.9 to 0.9
Outputs:
- vectors: float32 [128, 3, 32, 1024], P(None, None, 'rows', 'mode')
The draws below stay inside these ranges and needn't reach their ends.
Inputs may be any that keep to these rules, and one draw needn't show every extreme that they name: `owner_order`: every checkpoint slot is named by exactly one step.
All inputs are finite; a program needn't handle non-finite values. No bound on the sum of `land_mask` on one device may be relied on, other than what follows from the above.
Results may differ from the reference program's by a relative error of at most 0.0002.
Values sent between devices are 32-bit elements; how exact they have to be, the bound alone decides.
A program may use at most 64 MiB of HBM per device.

```python
import jax
import jax.numpy as jnp
from jax import lax

MODES = 128
NX = 1024
STEPS = 8
NY = 32


def touch_ends(entries, rng, low, largest):
    longest = entries.shape.index(max(entries.shape))
    spots = []
    for shift in (0, 1):
        where = [jax.random.randint(jax.random.fold_in(rng, axis), (), 0, length) for axis, length in enumerate(entries.shape)]
        where[longest] = (where[longest] + shift) % entries.shape[longest]
        spots.append(tuple(where))
    return entries.at[spots[0]].set(low).at[spots[1]].set(largest)


def levels(rng, extent, cuts, smallest, top_value):
    loudness = 1.0
    for dim, parts in cuts:
        steps = jax.random.uniform(jax.random.fold_in(jax.random.fold_in(rng, 6), dim), (parts,), jnp.float32, smallest / len(cuts), top_value / len(cuts))
        loudness = loudness * jnp.repeat(jnp.exp(steps), extent[dim] // parts).reshape((-1,) + (1,) * (len(extent) - 1 - dim))
    return loudness


def noise(stream_key, shape, spread, limit, split=(), kind=jnp.bfloat16):
    entries = spread * jax.random.normal(stream_key, shape, jnp.float32)
    if split:
        entries = entries * levels(stream_key, shape, split, -0.22, 0.18)
    return jnp.clip(entries, -limit, limit).astype(kind)


def setup_inputs(seed: int = 0) -> dict:
    streams_of = jax.random.split(jax.random.key(seed), 6)
    return {
        "tangents": noise(streams_of[0], (MODES, 3, NY, NX), 1.0, 6.0, ((0, 8), (2, 4)), jnp.float32),
        "checkpoints": jnp.clip(0.5 * jax.random.uniform(streams_of[1], (STEPS, 3, NY, NX), jnp.float32) ** levels(streams_of[1], (STEPS, 3, NY, NX), ((2, 4), (3, 8)), -0.2, 0.2), 0.0, 0.5),
        "owner_order": jax.random.permutation(streams_of[2], STEPS).astype(jnp.int32),
        "land_mask": touch_ends((jax.random.randint(streams_of[3], (NY, NX), 0, 5) < 4).astype(jnp.int32), jax.random.fold_in(streams_of[3], 1), 0, 1),
        "coefficients": noise(streams_of[4], (MODES, MODES), 0.15, 0.9, (), jnp.float32),
    }


mean_depth = 1.0
gravity = 1.0
coriolis = 0.5
time_step = 0.5


def deriv_x(values):
    return 0.5 * (jnp.roll(values, -1, -1) - jnp.roll(values, 1, -1))


def deriv_y(values):
    return 0.5 * (values[..., 2:, :] - values[..., :-2, :])


def interior(values):
    return values[..., 1:-1, :]


def tendency(base_flow, current):
    depth_total = mean_depth + base_flow[0]
    flow_u = base_flow[1]
    flow_v = base_flow[2]
    height = current[0]
    zonal = current[1]
    meridional = current[2]
    flux_x = depth_total * zonal + height * flow_u
    flux_y = depth_total * meridional + height * flow_v
    height_rate = -(interior(deriv_x(flux_x)) + deriv_y(flux_y))
    zonal_mid = interior(zonal)
    merid_mid = interior(meridional)
    flow_umid = interior(flow_u)
    flow_vmid = interior(flow_v)
    zonal_rate = -(flow_umid * interior(deriv_x(zonal)) + zonal_mid * interior(deriv_x(flow_u))
                   + flow_vmid * deriv_y(zonal) + merid_mid * deriv_y(flow_u)) + coriolis * merid_mid - gravity * interior(deriv_x(height))
    merid_rate = -(flow_umid * interior(deriv_x(meridional)) + zonal_mid * interior(deriv_x(flow_v))
                   + flow_vmid * deriv_y(meridional) + merid_mid * deriv_y(flow_v)) - coriolis * zonal_mid - gravity * deriv_y(height)
    return jnp.stack([height_rate, zonal_rate, merid_rate], 0)


def pad_rows(values):
    return jnp.pad(values, ((0, 0), (1, 1), (0, 0)))


def reference(tangents, checkpoints, owner_order, land_mask, coefficients):
    wet_mask = land_mask.astype(jnp.float32)

    def one_mode(initial):
        def advance(step_index, current):
            base_flow = lax.dynamic_index_in_dim(checkpoints, owner_order[step_index].astype(jnp.int32), 0, keepdims=False)
            padded_base = pad_rows(base_flow)
            slope_one = tendency(padded_base, pad_rows(current))
            middle = wet_mask * (current + time_step * slope_one)
            slope_two = tendency(padded_base, pad_rows(middle))
            return wet_mask * (current + 0.5 * time_step * (slope_one + slope_two))

        return lax.fori_loop(0, STEPS, advance, wet_mask * initial)

    final = lax.map(one_mode, tangents)
    mixing = jnp.eye(MODES, dtype=jnp.float32) + jnp.triu(coefficients)
    flattened = final.reshape(MODES, -1)
    mixed = jnp.dot(mixing.T, flattened, precision=lax.Precision.HIGHEST, preferred_element_type=jnp.float32)
    return mixed.reshape(final.shape)
```

```python
import functools

import jax
import jax.numpy as jnp
from jax import lax
from jax.experimental import pallas as pl
from jax.experimental.pallas import tpu as pltpu
from jax.sharding import PartitionSpec as P

mean_depth = 1.0
gravity = 1.0
coriolis = 0.5
time_step = 0.5


def padded(cells, sides, width):
    for axis, dim in sides:
        count = lax.axis_size(axis)
        ends = count - 1
        head = lax.slice_in_dim(cells, 0, width, axis=dim)
        tail = lax.slice_in_dim(cells, cells.shape[dim] - width, cells.shape[dim], axis=dim)
        cells = jnp.concatenate(
            [
                lax.ppermute(tail, axis, [(i, (i + 1) % count) for i in range(ends)]),
                cells,
                lax.ppermute(head, axis, [((i + 1) % count, i) for i in range(ends)]),
            ],
            axis=dim,
        )
    return cells


def deriv_x(values):
    return 0.5 * (jnp.roll(values, -1, -1) - jnp.roll(values, 1, -1))


def deriv_y(values):
    return 0.5 * (values[..., 2:, :] - values[..., :-2, :])


def interior(values):
    return values[..., 1:-1, :]


def tendency(base_flow, current):
    depth_total = mean_depth + base_flow[0]
    flow_u = base_flow[1]
    flow_v = base_flow[2]
    height = current[:, 0]
    zonal = current[:, 1]
    meridional = current[:, 2]
    flux_x = depth_total * zonal + height * flow_u
    flux_y = depth_total * meridional + height * flow_v
    height_rate = -(interior(deriv_x(flux_x)) + deriv_y(flux_y))
    zonal_mid = interior(zonal)
    merid_mid = interior(meridional)
    flow_umid = interior(flow_u)
    flow_vmid = interior(flow_v)
    zonal_rate = (
        -(
            flow_umid * interior(deriv_x(zonal))
            + zonal_mid * interior(deriv_x(flow_u))
            + flow_vmid * deriv_y(zonal)
            + merid_mid * deriv_y(flow_u)
        )
        + coriolis * merid_mid
        - gravity * interior(deriv_x(height))
    )
    merid_rate = (
        -(
            flow_umid * interior(deriv_x(meridional))
            + zonal_mid * interior(deriv_x(flow_v))
            + flow_vmid * deriv_y(meridional)
            + merid_mid * deriv_y(flow_v)
        )
        - coriolis * zonal_mid
        - gravity * deriv_y(height)
    )
    return jnp.stack([height_rate, zonal_rate, merid_rate], 1)


def step_wide(base_wide, state_wide, wet_wide):
    slope_one = tendency(base_wide, state_wide)
    middle = wet_wide[1:-1] * (state_wide[:, :, 1:-1] + time_step * slope_one)
    slope_two = tendency(base_wide[:, 1:-1], middle)
    return wet_wide[2:-2] * (
        state_wide[:, :, 2:-2] + 0.5 * time_step * (slope_one[:, :, 1:-1] + slope_two)
    )


def on_device_general(tangents, checkpoints, owner_order, land_mask, coefficients):
    wet_mask = land_mask.astype(jnp.float32)
    current = wet_mask * tangents
    depth = 2
    flows_wide, wet_stack = (
        padded(checkpoints, (("rows", 2),), depth),
        padded(wet_mask[None, None], (("rows", 2),), depth),
    )
    wet_wide = wet_stack[0, 0]

    def fetch_flow(step_index):
        held_tile = lax.dynamic_index_in_dim(flows_wide, owner_order[step_index], 0, keepdims=False)
        return lax.all_gather(held_tile, "mode", axis=2, tiled=True)

    total_steps = owner_order.shape[0]

    def advance(step_index, current):
        widened = padded(current, (("rows", 2),), 2)
        return step_wide(fetch_flow(step_index), widened, wet_wide)

    final = lax.fori_loop(0, total_steps, advance, current)
    mixing = jnp.eye(coefficients.shape[0], dtype=jnp.float32) + jnp.triu(coefficients)
    cell_block = lax.all_to_all(final, "mode", split_axis=3, concat_axis=0, tiled=True)
    flattened = cell_block.reshape(cell_block.shape[0], -1)
    mixed = jnp.dot(
        mixing.T, flattened, precision=lax.Precision.HIGHEST, preferred_element_type=jnp.float32
    )
    return mixed.reshape(cell_block.shape)


LANES = 128
SUB = 8
COEFS = 7


def tile_shift(values, lane, ahead):
    tiles = values.shape[0]
    if ahead:
        rolled = pltpu.roll(values, LANES - 1, 2)
        beside = jnp.concatenate([rolled[1:], rolled[:1]], axis=0) if tiles > 1 else rolled
        return jnp.where(lane == LANES - 1, beside, rolled)
    rolled = pltpu.roll(values, 1, 2)
    beside = jnp.concatenate([rolled[-1:], rolled[:-1]], axis=0) if tiles > 1 else rolled
    return jnp.where(lane == 0, beside, rolled)


def diff_x(values, lane):
    return tile_shift(values, lane, True) - tile_shift(values, lane, False)


def zero_pads(ref, strips):
    lead = ref.shape[:-2]
    edge = jnp.zeros(lead + (SUB, LANES), jnp.float32)
    ref[..., pl.ds(0, SUB), :] = edge
    ref[..., pl.ds(SUB * (strips + 1), SUB), :] = edge


def band(strip, shift=0):
    return pl.ds(SUB * (strip + 1) + shift, SUB)


def build_coefs(order, base_ref, coef, flow_pad, strips, steps, lane):
    zero_pads(flow_pad, strips)

    def one(step, carry):
        first = 3 * order[step]
        for strip in range(strips):
            coef[step, 0, :, pl.ds(SUB * strip, SUB), :] = 0.0625 * (
                mean_depth + base_ref[:, strip, first]
            )
            flow_pad[0, :, band(strip), :] = 0.25 * base_ref[:, strip, first + 1]
            flow_pad[1, :, band(strip), :] = 0.25 * base_ref[:, strip, first + 2]
        for strip in range(strips):
            rows = pl.ds(SUB * strip, SUB)
            flow_u = flow_pad[0, :, band(strip), :]
            flow_v = flow_pad[1, :, band(strip), :]
            coef[step, 1, :, rows, :] = flow_u
            coef[step, 2, :, rows, :] = flow_v
            coef[step, 3, :, rows, :] = diff_x(flow_u, lane)
            coef[step, 4, :, rows, :] = 0.25 - (
                flow_pad[0, :, band(strip, 1), :] - flow_pad[0, :, band(strip, -1), :]
            )
            coef[step, 5, :, rows, :] = 0.25 + diff_x(flow_v, lane)
            coef[step, 6, :, rows, :] = (
                flow_pad[1, :, band(strip, 1), :] - flow_pad[1, :, band(strip, -1), :]
            )
        return carry

    lax.fori_loop(0, steps, one, 0)


def store_flux(source, flux, coef, step, strip):
    rows = pl.ds(SUB * strip, SUB)
    flux[:, band(strip), :] = (
        coef[step, 0, :, rows, :] * source[2, :, band(strip), :]
        + coef[step, 2, :, rows, :] * source[0, :, band(strip), :]
    )


def scaled_rates(source, flux, coef, step, strip, lane):
    rows = pl.ds(SUB * strip, SUB)
    here, above, below = band(strip), band(strip, 1), band(strip, -1)
    height, zonal, merid = source[0, :, here, :], source[1, :, here, :], source[2, :, here, :]
    depth, flow_u, flow_v, du_dx, turn_v, turn_u, dv_dy = (
        coef[step, i, :, rows, :] for i in range(COEFS)
    )
    flux_x = depth * zonal + flow_u * height
    rate_h = diff_x(flux_x, lane) + (flux[:, above, :] - flux[:, below, :])
    rate_u = turn_v * merid - (
        flow_u * diff_x(zonal, lane)
        + du_dx * zonal
        + flow_v * (source[1, :, above, :] - source[1, :, below, :])
        + diff_x(height, lane)
    )
    rate_v = (
        flow_u * diff_x(merid, lane)
        + turn_u * zonal
        + flow_v * (source[2, :, above, :] - source[2, :, below, :])
        + dv_dy * merid
        + (source[0, :, above, :] - source[0, :, below, :])
    )
    return (height, zonal, merid), (-rate_h, rate_u, -rate_v)


def run_steps(state, middle, flux, coef, wet, strips, steps, lane):
    def one(step, carry):
        for strip in range(strips):
            store_flux(state, flux, coef, step, strip)
        for strip in range(strips):
            held, rates = scaled_rates(state, flux, coef, step, strip, lane)
            water = wet[:, pl.ds(SUB * strip, SUB), :]
            for f in range(3):
                middle[f, :, band(strip), :] = water * (held[f] + rates[f])
        for strip in range(strips):
            store_flux(middle, flux, coef, step, strip)
        for strip in range(strips):
            held, rates = scaled_rates(middle, flux, coef, step, strip, lane)
            water = wet[:, pl.ds(SUB * strip, SUB), :]
            for f in range(3):
                state[f, :, band(strip), :] = state[f, :, band(strip), :] + water * (
                    held[f] + rates[f]
                )
        return carry

    lax.fori_loop(0, steps, one, 0)


def steps_kernel(strips, tiles, steps, kept, order_ref, base_ref, land_ref, tan_ref, out_ref,
                 base_all, whole, leaving, coef, wet, state, middle, flux, flow_pad,
                 z_send, z_recv, x_send, x_recv, p_send, p_recv,
                 in_send, in_recv, out_send, out_recv, line, plane, half_in, cross,
                 land, order, fetch):
    m = lax.axis_index("mode")
    r = lax.axis_index("rows")
    everyone = tiles * strips
    me = m * strips + r
    chips = tiles // 2
    pairs = 2 * (m // 2)
    core = m - pairs
    partner = pairs + 1 - core
    mask_at = 3 * steps
    lane = lax.broadcasted_iota(jnp.int32, (tiles, SUB, LANES), 2)

    def other_chip(j):
        return lax.rem(m + 2 * j, tiles)

    def send(source, target, sent, received, mode, row):
        pltpu.make_async_remote_copy(
            src_ref=source, dst_ref=target, send_sem=sent, recv_sem=received,
            device_id=(mode, row), device_id_type=pl.DeviceIdType.MESH,
        ).start()

    def drain(ref, sem):
        pltpu.make_async_copy(ref, ref, sem).wait()

    barrier = pltpu.get_barrier_semaphore()
    half = strips // 2
    upper = r >= half
    at_end = jnp.logical_or(r == 0, r == strips - 1)
    at_mid = jnp.logical_or(r == half - 1, r == half)
    not_end, not_mid = jnp.logical_not(at_end), jnp.logical_not(at_mid)
    inner = jnp.where(upper, r - 1, r + 1)
    outer = jnp.where(upper, r + 1, r - 1)

    def signal(sem, mode, row):
        pl.semaphore_signal(
            sem, inc=1, device_id=(mode, row), device_id_type=pl.DeviceIdType.MESH
        )

    def signal_plane(sem):
        for j in range(1, tiles):
            signal(sem, lax.rem(m + j, tiles), r)

    def sibling(i):
        return jnp.where(upper, half + lax.rem(r + i, half), lax.rem(r + i, half))

    def opposite(i):
        return jnp.where(upper, half - 1 - i, half + i)

    @pl.when(at_mid)
    def _():
        signal(barrier, m, inner)

    @pl.when(jnp.logical_and(at_mid, not_end))
    def _():
        signal(barrier, m, outer)

    @pl.when(at_end)
    def _():
        signal_plane(barrier)

    own = base_all.at[m, r]
    tile_of_land = land_ref.at[:, pl.ds(pl.multiple_of(m * LANES, LANES), LANES)]
    fetch_base = pltpu.make_async_copy(base_ref, own.at[pl.ds(0, mask_at)], fetch.at[0])
    fetch_land = pltpu.make_async_copy(tile_of_land, land, fetch.at[1])
    fetch_order = pltpu.make_async_copy(order_ref, order, fetch.at[2])
    fetch_land.start()
    fetch_base.start()
    fetch_order.start()

    @pl.when(at_end)
    def _():
        pl.semaphore_wait(barrier, tiles)

    @pl.when(not_end)
    def _():
        pl.semaphore_wait(barrier, 1)

    if half > 2:

        @pl.when(jnp.logical_and(not_end, not_mid))
        def _():
            signal(barrier, m, outer)

    def send_in(k, q):
        send(tan_ref.at[q * kept + k], whole.at[k, r], in_send, in_recv.at[k], m, q)

    def pass_up(q):
        strip = base_all.at[m, q]
        send(strip, strip, z_send.at[0, q], z_recv.at[q], m, r + 1)

    def pass_down(q):
        strip = base_all.at[m, q]
        send(strip, strip, z_send.at[1, q], z_recv.at[q], m, r - 1)

    def spread(q):
        strip = base_all.at[m, q]
        for j in range(1, chips):
            send(strip, strip, x_send, x_recv.at[m], other_chip(j), r)

    early = min(2, kept)
    lead = 2
    send_in(0, inner)
    fetch_land.wait()
    own[mask_at] = land[...].astype(jnp.float32)
    fetch_base.wait()
    fetch_order.wait()

    @pl.when(upper)
    def _():
        pass_down(r)

    @pl.when(jnp.logical_not(upper))
    def _():
        pass_up(r)

    for k in range(1, early):
        send_in(k, inner)

    @pl.when(not_mid)
    def _():
        signal(line, m, inner)

    @pl.when(at_end)
    def _():
        signal_plane(plane)
        spread(r)

    @pl.when(not_end)
    def _():
        pl.semaphore_wait(line, 1)

        @pl.when(upper)
        def _():
            pass_up(r)

        @pl.when(jnp.logical_not(upper))
        def _():
            pass_down(r)

        send_in(0, outer)

    @pl.when(at_end)
    def _():
        pl.semaphore_wait(plane, tiles - 1)
        for i in range(1, half):
            signal(half_in, m, sibling(i))

    @pl.when(not_end)
    def _():
        pl.semaphore_wait(half_in, 1)
        spread(r)

    @pl.when(at_mid)
    def _():
        signal(cross, m, inner)
        pl.semaphore_wait(cross, 1)
        for i in range(1, half):
            signal(cross, m, sibling(i))

    def send_rest(k):
        for i in range(half):
            q = opposite(i)
            if k < early:

                @pl.when(q != inner)
                def _():
                    send_in(k, q)
            else:
                send_in(k, q)
        for i in range(1, half):
            q = sibling(i)
            if k < early:
                done = q == inner
                if k == 0:
                    done = jnp.logical_or(done, q == outer)

                @pl.when(jnp.logical_not(done))
                def _():
                    send_in(k, q)
            else:
                send_in(k, q)

    def relay(q):

        @pl.when(jnp.logical_and(q < r, r < strips - 1))
        def _():
            pass_up(q)

        @pl.when(jnp.logical_and(q > r, r > 0))
        def _():
            pass_down(q)

        spread(q)

    for j in range(1, strips):

        @pl.when(r >= j)
        def _():
            drain(base_all.at[m, r - j], z_recv.at[r - j])
            relay(r - j)

        @pl.when(r + j < strips)
        def _():
            drain(base_all.at[m, r + j], z_recv.at[r + j])
            relay(r + j)

        if j == 1:

            @pl.when(not_mid)
            def _():
                pl.semaphore_wait(cross, 1)

            send_rest(0)

    for k in range(kept):
        if k > 0:
            send_rest(k)
        pltpu.make_async_copy(tan_ref.at[r * kept + k], whole.at[k, r], in_recv.at[k]).start()
    send(base_all.at[m], base_all.at[m], p_send, p_recv, partner, r)
    for ref in (state, middle, flux):
        zero_pads(ref, strips)
    for j in range(1, chips):
        tile = other_chip(j)
        drain(base_all.at[tile], x_recv.at[tile])
        send(base_all.at[tile], base_all.at[tile], p_send, p_recv, partner, r)
    drain(base_all.at[pl.ds(0, chips)], p_recv)

    for strip in range(strips):
        wet[:, pl.ds(SUB * strip, SUB), :] = base_all[:, strip, mask_at]
    build_coefs(order, base_all, coef, flow_pad, strips, steps, lane)

    def one_mode(k, carry):
        drain(whole.at[k], in_recv.at[k])
        for f, scale in enumerate((0.25, 1.0, 1.0)):
            for strip in range(strips):
                for t in range(tiles):
                    state[f, t, band(strip), :] = (
                        scale * wet[t, pl.ds(SUB * strip, SUB), :]
                    ) * whole[k, strip, f, :, pl.ds(LANES * t, LANES)]
        run_steps(state, middle, flux, coef, wet, strips, steps, lane)
        down = 0.5 ** steps
        for f, scale in enumerate((4.0 * down, down, down)):
            for strip in range(strips):
                for t in range(tiles):
                    leaving[k, t * strips + strip, f] = scale * state[f, t, band(strip), :]

        def post(row, mode):
            send(leaving.at[k, mode * strips + row], out_ref.at[me, k], out_send, out_recv, mode, row)

        def post_row(row):
            for first in range(lead):

                @pl.when(jnp.logical_and(row == 0, jnp.logical_or(r != 0, m != first)))
                def _():
                    post(row, first)

            def to(j, carry):
                mode = lax.rem(m + j, tiles)

                @pl.when(jnp.logical_and(
                    jnp.logical_or(row != r, mode != m), jnp.logical_or(row != 0, mode >= lead)
                ))
                def _():
                    post(row, mode)

                return carry

            lax.fori_loop(0, tiles, to, 0)

        for i in range(half):
            post_row(opposite(half - 1 - i))
        for i in range(1, half):
            post_row(sibling(i))
        post_row(r)
        pltpu.make_async_copy(leaving.at[k, me], out_ref.at[me, k], out_recv).start()
        return carry

    lax.fori_loop(0, kept, one_mode, 0)

    for q in range(strips):

        @pl.when(jnp.logical_and(q <= r, r < strips - 1))
        def _():
            drain(base_all.at[m, q], z_send.at[0, q])

        @pl.when(jnp.logical_and(q >= r, r > 0))
        def _():
            drain(base_all.at[m, q], z_send.at[1, q])

    drain(base_all.at[pl.ds(0, chips - 1)], x_send)
    drain(base_all.at[pl.ds(0, chips)], p_send)
    drain(whole.at[:, pl.ds(0, strips - 1)], in_send)
    drain(leaving.at[:, pl.ds(0, everyone - 1)], out_send)
    drain(out_ref, out_recv)


def step_modes(order, base, land, tangents):
    strips, tiles = lax.axis_size("rows"), lax.axis_size("mode")
    held, fields, rows, columns = tangents.shape
    steps = base.shape[0]
    kept = held // strips
    everyone = tiles * strips
    tall = SUB * (strips + 2)
    hbm = pl.BlockSpec(memory_space=pltpu.HBM)
    operands = (order, base.reshape(steps * fields, rows, LANES), land, tangents)
    dma, regular = pltpu.SemaphoreType.DMA, pltpu.SemaphoreType.REGULAR
    return pl.pallas_call(
        functools.partial(steps_kernel, strips, tiles, steps, kept),
        out_shape=jax.ShapeDtypeStruct((everyone, kept, fields, rows, LANES), jnp.float32),
        in_specs=[hbm] * 4,
        out_specs=pl.BlockSpec(memory_space=pl.ANY),
        scratch_shapes=[
            pltpu.VMEM((tiles, strips, steps * fields + 1, rows, LANES), jnp.float32),
            pltpu.VMEM((kept, strips, fields, rows, columns), jnp.float32),
            pltpu.VMEM((kept, everyone, fields, rows, LANES), jnp.float32),
            pltpu.VMEM((steps, COEFS, tiles, SUB * strips, LANES), jnp.float32),
            pltpu.VMEM((tiles, SUB * strips, LANES), jnp.float32),
            pltpu.VMEM((3, tiles, tall, LANES), jnp.float32),
            pltpu.VMEM((3, tiles, tall, LANES), jnp.float32),
            pltpu.VMEM((tiles, tall, LANES), jnp.float32),
            pltpu.VMEM((2, tiles, tall, LANES), jnp.float32),
            dma((2, strips)), dma((strips,)), dma, dma((tiles,)), dma, dma,
            dma, dma((kept,)), dma, dma,
            regular, regular, regular, regular,
            pltpu.VMEM((rows, LANES), jnp.int32), pltpu.SMEM((steps,), jnp.int32), dma((3,)),
        ],
        compiler_params=pltpu.CompilerParams(
            collective_id=0, has_side_effects=True, vmem_limit_bytes=24 << 20
        ),
    )(*(pltpu.with_memory_space_constraint(held_in_hbm, pltpu.HBM) for held_in_hbm in operands))


def halves(values):
    high = values.astype(jnp.bfloat16)
    return high, (values - high.astype(jnp.float32)).astype(jnp.bfloat16)


def mix_kernel(coef_ref, cells_ref, out_ref, staged, sems):
    modes, spots, _ = cells_ref.shape
    row = lax.broadcasted_iota(jnp.int32, (modes, modes), 0)
    col = lax.broadcasted_iota(jnp.int32, (modes, modes), 1)
    mixing = jnp.where(row <= col, coef_ref[...], 0.0) + jnp.where(row == col, 1.0, 0.0)
    high, low = halves(mixing.T)
    turned = jnp.concatenate(
        [jnp.concatenate([high, high], 1), jnp.concatenate([low, low], 1)], 0
    )
    cells = cells_ref.reshape(modes * spots, LANES)
    copies = []
    for group in range(spots // SUB):
        out = staged.at[group].reshape(modes * SUB, LANES)
        for spot in range(0, SUB, 2):
            first = SUB * group + spot
            high, low = halves(jnp.concatenate(
                [cells[pl.ds(first + i, modes, stride=spots), :] for i in (0, 1)], 1
            ))
            mixed = jnp.dot(
                turned, jnp.concatenate([high, low], 0), preferred_element_type=jnp.float32
            )
            mixed = mixed[:modes] + mixed[modes:]
            for i in (0, 1):
                out[pl.ds(spot + i, modes, stride=SUB), :] = mixed[:, LANES * i:LANES * (i + 1)]
        copies.append(pltpu.make_async_copy(
            staged.at[group], out_ref.at[:, pl.ds(SUB * group, SUB)], sems.at[group]
        ))
        copies[-1].start()
    for copy in copies:
        copy.wait()


def mix(coefficients, cells):
    modes, spots, _ = cells.shape
    return pl.pallas_call(
        mix_kernel,
        out_shape=jax.ShapeDtypeStruct(cells.shape, jnp.float32),
        in_specs=[pl.BlockSpec(memory_space=pltpu.VMEM)] * 2,
        out_specs=pl.BlockSpec(memory_space=pltpu.HBM),
        scratch_shapes=[
            pltpu.VMEM((spots // SUB, modes, SUB, LANES), jnp.float32),
            pltpu.SemaphoreType.DMA((spots // SUB,)),
        ],
        compiler_params=pltpu.CompilerParams(vmem_limit_bytes=8 << 20),
    )(coefficients, cells)


def on_device_whole(tangents, checkpoints, owner_order, land_mask, coefficients):
    fields, rows = tangents.shape[1:3]
    placed = step_modes(owner_order, checkpoints, land_mask, tangents)
    mixed = mix(coefficients, placed.reshape(coefficients.shape[0], fields * rows, LANES))
    return mixed.reshape(coefficients.shape[0], fields, rows, LANES)


def on_device(tangents, checkpoints, owner_order, land_mask, coefficients):
    strips = lax.axis_size("rows")
    held, _, rows, columns = tangents.shape
    fits = (
        held % strips == 0 and strips % 2 == 0 and lax.axis_size("mode") % 2 == 0
        and lax.axis_size("mode") > 2 and rows == SUB and checkpoints.shape[-1] == LANES and strips <= 8
        and coefficients.shape[0] % LANES == 0
    )
    chosen = on_device_whole if fits else on_device_general
    return chosen(tangents, checkpoints, owner_order, land_mask, coefficients)


def solution(mesh):
    placed = (
        P("mode", None, "rows", None),
        P(None, None, "rows", "mode"),
        P(),
        P("rows", None),
        P(),
    )
    return jax.shard_map(
        on_device,
        mesh=mesh,
        in_specs=placed,
        out_specs=P(None, None, "rows", "mode"),
        check_vma=False,
    )
```

```python
import functools

import jax
import jax.numpy as jnp
from jax import lax
from jax.experimental import pallas as pl
from jax.experimental.pallas import tpu as pltpu
from jax.sharding import PartitionSpec as P

mean_depth = 1.0
gravity = 1.0
coriolis = 0.5
time_step = 0.5


def padded(cells, sides, width):
    for axis, dim in sides:
        count = lax.axis_size(axis)
        ends = count - 1
        head = lax.slice_in_dim(cells, 0, width, axis=dim)
        tail = lax.slice_in_dim(cells, cells.shape[dim] - width, cells.shape[dim], axis=dim)
        cells = jnp.concatenate(
            [
                lax.ppermute(tail, axis, [(i, (i + 1) % count) for i in range(ends)]),
                cells,
                lax.ppermute(head, axis, [((i + 1) % count, i) for i in range(ends)]),
            ],
            axis=dim,
        )
    return cells


def deriv_x(values):
    return 0.5 * (jnp.roll(values, -1, -1) - jnp.roll(values, 1, -1))


def deriv_y(values):
    return 0.5 * (values[..., 2:, :] - values[..., :-2, :])


def interior(values):
    return values[..., 1:-1, :]


def tendency(base_flow, current):
    depth_total = mean_depth + base_flow[0]
    flow_u = base_flow[1]
    flow_v = base_flow[2]
    height = current[:, 0]
    zonal = current[:, 1]
    meridional = current[:, 2]
    flux_x = depth_total * zonal + height * flow_u
    flux_y = depth_total * meridional + height * flow_v
    height_rate = -(interior(deriv_x(flux_x)) + deriv_y(flux_y))
    zonal_mid = interior(zonal)
    merid_mid = interior(meridional)
    flow_umid = interior(flow_u)
    flow_vmid = interior(flow_v)
    zonal_rate = (
        -(
            flow_umid * interior(deriv_x(zonal))
            + zonal_mid * interior(deriv_x(flow_u))
            + flow_vmid * deriv_y(zonal)
            + merid_mid * deriv_y(flow_u)
        )
        + coriolis * merid_mid
        - gravity * interior(deriv_x(height))
    )
    merid_rate = (
        -(
            flow_umid * interior(deriv_x(meridional))
            + zonal_mid * interior(deriv_x(flow_v))
            + flow_vmid * deriv_y(meridional)
            + merid_mid * deriv_y(flow_v)
        )
        - coriolis * zonal_mid
        - gravity * deriv_y(height)
    )
    return jnp.stack([height_rate, zonal_rate, merid_rate], 1)


def step_wide(base_wide, state_wide, wet_wide):
    slope_one = tendency(base_wide, state_wide)
    middle = wet_wide[1:-1] * (state_wide[:, :, 1:-1] + time_step * slope_one)
    slope_two = tendency(base_wide[:, 1:-1], middle)
    return wet_wide[2:-2] * (
        state_wide[:, :, 2:-2] + 0.5 * time_step * (slope_one[:, :, 1:-1] + slope_two)
    )


def on_device_general(tangents, checkpoints, owner_order, land_mask, coefficients):
    wet_mask = land_mask.astype(jnp.float32)
    current = wet_mask * tangents
    depth = 2
    flows_wide, wet_stack = (
        padded(checkpoints, (("rows", 2),), depth),
        padded(wet_mask[None, None], (("rows", 2),), depth),
    )
    wet_wide = wet_stack[0, 0]

    def fetch_flow(step_index):
        held_tile = lax.dynamic_index_in_dim(flows_wide, owner_order[step_index], 0, keepdims=False)
        return lax.all_gather(held_tile, "mode", axis=2, tiled=True)

    total_steps = owner_order.shape[0]

    def advance(step_index, current):
        widened = padded(current, (("rows", 2),), 2)
        return step_wide(fetch_flow(step_index), widened, wet_wide)

    final = lax.fori_loop(0, total_steps, advance, current)
    mixing = jnp.eye(coefficients.shape[0], dtype=jnp.float32) + jnp.triu(coefficients)
    cell_block = lax.all_to_all(final, "mode", split_axis=3, concat_axis=0, tiled=True)
    flattened = cell_block.reshape(cell_block.shape[0], -1)
    mixed = jnp.dot(
        mixing.T, flattened, precision=lax.Precision.HIGHEST, preferred_element_type=jnp.float32
    )
    return mixed.reshape(cell_block.shape)


LANES = 128
SUB = 8
COEFS = 7


def tile_shift(values, lane, ahead):
    tiles = values.shape[0]
    if ahead:
        rolled = pltpu.roll(values, LANES - 1, 2)
        beside = jnp.concatenate([rolled[1:], rolled[:1]], axis=0) if tiles > 1 else rolled
        return jnp.where(lane == LANES - 1, beside, rolled)
    rolled = pltpu.roll(values, 1, 2)
    beside = jnp.concatenate([rolled[-1:], rolled[:-1]], axis=0) if tiles > 1 else rolled
    return jnp.where(lane == 0, beside, rolled)


def diff_x(values, lane):
    return tile_shift(values, lane, True) - tile_shift(values, lane, False)


def zero_pads(ref, strips):
    lead = ref.shape[:-2]
    edge = jnp.zeros(lead + (SUB, LANES), jnp.float32)
    ref[..., pl.ds(0, SUB), :] = edge
    ref[..., pl.ds(SUB * (strips + 1), SUB), :] = edge


def band(strip, shift=0):
    return pl.ds(SUB * (strip + 1) + shift, SUB)


def build_coefs(order, base_ref, coef, flow_pad, strips, steps, lane):
    zero_pads(flow_pad, strips)

    def one(step, carry):
        first = 3 * order[step]
        for strip in range(strips):
            coef[step, 0, :, pl.ds(SUB * strip, SUB), :] = 0.0625 * (
                mean_depth + base_ref[:, strip, first]
            )
            flow_pad[0, :, band(strip), :] = 0.25 * base_ref[:, strip, first + 1]
            flow_pad[1, :, band(strip), :] = 0.25 * base_ref[:, strip, first + 2]
        for strip in range(strips):
            rows = pl.ds(SUB * strip, SUB)
            flow_u = flow_pad[0, :, band(strip), :]
            flow_v = flow_pad[1, :, band(strip), :]
            coef[step, 1, :, rows, :] = flow_u
            coef[step, 2, :, rows, :] = flow_v
            coef[step, 3, :, rows, :] = diff_x(flow_u, lane)
            coef[step, 4, :, rows, :] = 0.25 - (
                flow_pad[0, :, band(strip, 1), :] - flow_pad[0, :, band(strip, -1), :]
            )
            coef[step, 5, :, rows, :] = 0.25 + diff_x(flow_v, lane)
            coef[step, 6, :, rows, :] = (
                flow_pad[1, :, band(strip, 1), :] - flow_pad[1, :, band(strip, -1), :]
            )
        return carry

    lax.fori_loop(0, steps, one, 0)


def store_flux(source, flux, coef, step, strip):
    rows = pl.ds(SUB * strip, SUB)
    flux[:, band(strip), :] = (
        coef[step, 0, :, rows, :] * source[2, :, band(strip), :]
        + coef[step, 2, :, rows, :] * source[0, :, band(strip), :]
    )


def scaled_rates(source, flux, coef, step, strip, lane):
    rows = pl.ds(SUB * strip, SUB)
    here, above, below = band(strip), band(strip, 1), band(strip, -1)
    height, zonal, merid = source[0, :, here, :], source[1, :, here, :], source[2, :, here, :]
    depth, flow_u, flow_v, du_dx, turn_v, turn_u, dv_dy = (
        coef[step, i, :, rows, :] for i in range(COEFS)
    )
    flux_x = depth * zonal + flow_u * height
    rate_h = diff_x(flux_x, lane) + (flux[:, above, :] - flux[:, below, :])
    rate_u = turn_v * merid - (
        flow_u * diff_x(zonal, lane)
        + du_dx * zonal
        + flow_v * (source[1, :, above, :] - source[1, :, below, :])
        + diff_x(height, lane)
    )
    rate_v = (
        flow_u * diff_x(merid, lane)
        + turn_u * zonal
        + flow_v * (source[2, :, above, :] - source[2, :, below, :])
        + dv_dy * merid
        + (source[0, :, above, :] - source[0, :, below, :])
    )
    return (height, zonal, merid), (-rate_h, rate_u, -rate_v)


def run_steps(state, middle, flux, coef, wet, strips, steps, lane):
    def one(step, carry):
        for strip in range(strips):
            store_flux(state, flux, coef, step, strip)
        for strip in range(strips):
            held, rates = scaled_rates(state, flux, coef, step, strip, lane)
            water = wet[:, pl.ds(SUB * strip, SUB), :]
            for f in range(3):
                middle[f, :, band(strip), :] = water * (held[f] + rates[f])
        for strip in range(strips):
            store_flux(middle, flux, coef, step, strip)
        for strip in range(strips):
            held, rates = scaled_rates(middle, flux, coef, step, strip, lane)
            water = wet[:, pl.ds(SUB * strip, SUB), :]
            for f in range(3):
                state[f, :, band(strip), :] = state[f, :, band(strip), :] + water * (
                    held[f] + rates[f]
                )
        return carry

    lax.fori_loop(0, steps, one, 0)


def steps_kernel(strips, tiles, steps, kept, order_ref, base_ref, land_ref, tan_ref, out_ref,
                 base_all, whole, leaving, coef, wet, state, middle, flux, flow_pad,
                 z_send, z_recv, x_send, x_recv, p_send, p_recv,
                 in_send, in_recv, out_send, out_recv, line, plane, half_in, cross,
                 land, order, fetch):
    m = lax.axis_index("mode")
    r = lax.axis_index("rows")
    everyone = tiles * strips
    me = m * strips + r
    chips = tiles // 2
    pairs = 2 * (m // 2)
    core = m - pairs
    partner = pairs + 1 - core
    mask_at = 3 * steps
    lane = lax.broadcasted_iota(jnp.int32, (tiles, SUB, LANES), 2)

    def other_chip(j):
        return lax.rem(m + 2 * j, tiles)

    def send(source, target, sent, received, mode, row):
        pltpu.make_async_remote_copy(
            src_ref=source, dst_ref=target, send_sem=sent, recv_sem=received,
            device_id=(mode, row), device_id_type=pl.DeviceIdType.MESH,
        ).start()

    def beside(step):
        chip, target, bit = m // 2, 0, 1
        if chips & (chips - 1):
            return lax.rem(chip + step, chips)
        while bit < chips:
            target = target + bit * ((chip // bit + step // bit) % 2)
            bit = 2 * bit
        return target

    farthest_first = []
    for step in reversed(range(chips)):
        chip_there = beside(step)
        farthest_first += [2 * chip_there + 1 - core, 2 * chip_there + core]

    def drain(ref, sem):
        pltpu.make_async_copy(ref, ref, sem).wait()

    barrier = pltpu.get_barrier_semaphore()
    half = strips // 2
    upper = r >= half
    at_end = jnp.logical_or(r == 0, r == strips - 1)
    at_mid = jnp.logical_or(r == half - 1, r == half)
    not_end, not_mid = jnp.logical_not(at_end), jnp.logical_not(at_mid)
    inner = jnp.where(upper, r - 1, r + 1)
    outer = jnp.where(upper, r + 1, r - 1)

    def signal(sem, mode, row):
        pl.semaphore_signal(
            sem, inc=1, device_id=(mode, row), device_id_type=pl.DeviceIdType.MESH
        )

    def signal_plane(sem):
        for j in range(1, tiles):
            signal(sem, lax.rem(m + j, tiles), r)

    def sibling(i):
        return jnp.where(upper, half + lax.rem(r + i, half), lax.rem(r + i, half))

    def opposite(i):
        return jnp.where(upper, half - 1 - i, half + i)

    @pl.when(at_mid)
    def _():
        signal(barrier, m, inner)

    @pl.when(jnp.logical_and(at_mid, not_end))
    def _():
        signal(barrier, m, outer)

    @pl.when(at_end)
    def _():
        signal_plane(barrier)

    own = base_all.at[m, r]
    tile_of_land = land_ref.at[:, pl.ds(pl.multiple_of(m * LANES, LANES), LANES)]
    fetch_base = pltpu.make_async_copy(base_ref, own.at[pl.ds(0, mask_at)], fetch.at[0])
    fetch_land = pltpu.make_async_copy(tile_of_land, land, fetch.at[1])
    fetch_order = pltpu.make_async_copy(order_ref, order, fetch.at[2])
    fetch_land.start()
    fetch_base.start()
    fetch_order.start()

    @pl.when(at_end)
    def _():
        pl.semaphore_wait(barrier, tiles)

    @pl.when(not_end)
    def _():
        pl.semaphore_wait(barrier, 1)

    if half > 2:

        @pl.when(jnp.logical_and(not_end, not_mid))
        def _():
            signal(barrier, m, outer)

    def send_in(k, q):
        send(tan_ref.at[q * kept + k], whole.at[k, r], in_send, in_recv.at[k], m, q)

    def pass_up(q):
        strip = base_all.at[m, q]
        send(strip, strip, z_send.at[0, q], z_recv.at[q], m, r + 1)

    def pass_down(q):
        strip = base_all.at[m, q]
        send(strip, strip, z_send.at[1, q], z_recv.at[q], m, r - 1)

    def spread(q):
        strip = base_all.at[m, q]
        for j in range(1, chips):
            send(strip, strip, x_send, x_recv.at[m], other_chip(j), r)

    def relay(q):

        @pl.when(jnp.logical_and(q < r, r < strips - 1))
        def _():
            pass_up(q)

        @pl.when(jnp.logical_and(q > r, r > 0))
        def _():
            pass_down(q)

        spread(q)

    def take_below(j):

        @pl.when(r >= j)
        def _():
            drain(base_all.at[m, r - j], z_recv.at[r - j])
            relay(r - j)

    def take_above(j):

        @pl.when(r + j < strips)
        def _():
            drain(base_all.at[m, r + j], z_recv.at[r + j])
            relay(r + j)

    def hop(j):
        @pl.when(upper)
        def _():
            take_above(j)

        take_below(j)

        @pl.when(jnp.logical_not(upper))
        def _():
            take_above(j)

    def send_near(k):
        send_in(k, opposite(0))

    def send_far(k):
        for i in range(1, half):
            send_in(k, opposite(i))

    def send_half(k):
        for i in range(1, half):
            send_in(k, sibling(i))

    modes = range(kept)

    @pl.when(at_mid)
    def _():
        send_near(0)

    fetch_land.wait()
    own[mask_at] = land[...].astype(jnp.float32)
    fetch_base.wait()
    fetch_order.wait()

    @pl.when(upper)
    def _():
        pass_down(r)

    @pl.when(jnp.logical_not(upper))
    def _():
        pass_up(r)

    @pl.when(not_mid)
    def _():
        signal(line, m, inner)

    @pl.when(at_end)
    def _():
        signal_plane(plane)
        spread(r)

    @pl.when(not_end)
    def _():
        pl.semaphore_wait(line, 1)

        @pl.when(upper)
        def _():
            pass_up(r)

        @pl.when(jnp.logical_not(upper))
        def _():
            pass_down(r)

    @pl.when(at_mid)
    def _():
        for k in modes[1:2]:
            send_near(k)

    @pl.when(at_end)
    def _():
        pl.semaphore_wait(plane, tiles - 1)
        for i in range(1, half):
            signal(half_in, m, sibling(i))

    @pl.when(not_end)
    def _():
        pl.semaphore_wait(half_in, 1)
        spread(r)

    @pl.when(at_mid)
    def _():
        signal(cross, m, inner)

    hop(1)
    send_half(0)

    @pl.when(at_mid)
    def _():
        pl.semaphore_wait(cross, 1)
        for i in range(1, half):
            signal(cross, m, sibling(i))
        for k in modes[2:]:
            send_near(k)

    for j in range(2, strips):
        hop(j)

    @pl.when(not_mid)
    def _():
        pl.semaphore_wait(cross, 1)

    def send_rest(far, near, beside):
        for k in far:
            send_far(k)

        @pl.when(not_mid)
        def _():
            for k in near:
                send_near(k)

        for k in beside:
            send_half(k)

    send_rest(modes[:1], modes[:2], modes[1:2])

    @pl.when(at_mid)
    def _():
        for k in modes[1:2]:
            send_far(k)

    for k in range(kept):
        pltpu.make_async_copy(tan_ref.at[r * kept + k], whole.at[k, r], in_recv.at[k]).start()
    send(base_all.at[m], base_all.at[m], p_send, p_recv, partner, r)
    for ref in (state, middle, flux):
        zero_pads(ref, strips)
    for j in range(1, chips):
        tile = other_chip(j)
        drain(base_all.at[tile], x_recv.at[tile])
        send(base_all.at[tile], base_all.at[tile], p_send, p_recv, partner, r)
    @pl.when(not_mid)
    def _():
        for k in modes[1:2]:
            send_far(k)

    send_rest((), modes[2:3], modes[2:3])
    drain(base_all.at[pl.ds(0, chips)], p_recv)
    send_rest(modes[2:], modes[3:], modes[3:])

    for strip in range(strips):
        wet[:, pl.ds(SUB * strip, SUB), :] = base_all[:, strip, mask_at]
    build_coefs(order, base_all, coef, flow_pad, strips, steps, lane)

    def one_mode(k, carry):
        drain(whole.at[k], in_recv.at[k])
        for f, scale in enumerate((0.25, 1.0, 1.0)):
            for strip in range(strips):
                for t in range(tiles):
                    state[f, t, band(strip), :] = (
                        scale * wet[t, pl.ds(SUB * strip, SUB), :]
                    ) * whole[k, strip, f, :, pl.ds(LANES * t, LANES)]
        run_steps(state, middle, flux, coef, wet, strips, steps, lane)
        down = 0.5 ** steps
        for f, scale in enumerate((4.0 * down, down, down)):
            for strip in range(strips):
                for t in range(tiles):
                    leaving[k, t * strips + strip, f] = scale * state[f, t, band(strip), :]

        for i in range(half):
            post_row(k, opposite(half - 1 - i))
        for i in range(1, half):
            post_row(k, sibling(i))
        post_row(k, r)
        pltpu.make_async_copy(leaving.at[k, me], out_ref.at[me, k], out_recv).start()
        return carry

    def post_row(k, row):
        def to(mode):
            send(leaving.at[k, mode * strips + row], out_ref.at[me, k], out_send, out_recv,
                 mode, row)

        for lead in (0, 1):

            @pl.when(jnp.logical_and(row == 0, jnp.logical_or(row != r, m != lead)))
            def _():
                to(lead)

        for mode in farthest_first:
            skip = jnp.logical_or(
                jnp.logical_and(row == r, mode == m), jnp.logical_and(row == 0, mode < 2)
            )

            @pl.when(jnp.logical_not(skip))
            def _():
                to(mode)

    lax.fori_loop(0, kept, one_mode, 0)

    for q in range(strips):

        @pl.when(jnp.logical_and(q <= r, r < strips - 1))
        def _():
            drain(base_all.at[m, q], z_send.at[0, q])

        @pl.when(jnp.logical_and(q >= r, r > 0))
        def _():
            drain(base_all.at[m, q], z_send.at[1, q])

    drain(base_all.at[pl.ds(0, chips - 1)], x_send)
    drain(base_all.at[pl.ds(0, chips)], p_send)
    drain(whole.at[:, pl.ds(0, strips - 1)], in_send)
    drain(leaving.at[:, pl.ds(0, everyone - 1)], out_send)
    drain(out_ref, out_recv)


def step_modes(order, base, land, tangents):
    strips, tiles = lax.axis_size("rows"), lax.axis_size("mode")
    held, fields, rows, columns = tangents.shape
    steps = base.shape[0]
    kept = held // strips
    everyone = tiles * strips
    tall = SUB * (strips + 2)
    hbm = pl.BlockSpec(memory_space=pltpu.HBM)
    operands = (order, base.reshape(steps * fields, rows, LANES), land, tangents)
    dma, regular = pltpu.SemaphoreType.DMA, pltpu.SemaphoreType.REGULAR
    return pl.pallas_call(
        functools.partial(steps_kernel, strips, tiles, steps, kept),
        out_shape=jax.ShapeDtypeStruct((everyone, kept, fields, rows, LANES), jnp.float32),
        in_specs=[hbm] * 4,
        out_specs=pl.BlockSpec(memory_space=pl.ANY),
        scratch_shapes=[
            pltpu.VMEM((tiles, strips, steps * fields + 1, rows, LANES), jnp.float32),
            pltpu.VMEM((kept, strips, fields, rows, columns), jnp.float32),
            pltpu.VMEM((kept, everyone, fields, rows, LANES), jnp.float32),
            pltpu.VMEM((steps, COEFS, tiles, SUB * strips, LANES), jnp.float32),
            pltpu.VMEM((tiles, SUB * strips, LANES), jnp.float32),
            pltpu.VMEM((3, tiles, tall, LANES), jnp.float32),
            pltpu.VMEM((3, tiles, tall, LANES), jnp.float32),
            pltpu.VMEM((tiles, tall, LANES), jnp.float32),
            pltpu.VMEM((2, tiles, tall, LANES), jnp.float32),
            dma((2, strips)), dma((strips,)), dma, dma((tiles,)), dma, dma,
            dma, dma((kept,)), dma, dma,
            regular, regular, regular, regular,
            pltpu.VMEM((rows, LANES), jnp.int32), pltpu.SMEM((steps,), jnp.int32), dma((3,)),
        ],
        compiler_params=pltpu.CompilerParams(
            collective_id=0, has_side_effects=True, vmem_limit_bytes=24 << 20
        ),
    )(*(pltpu.with_memory_space_constraint(held_in_hbm, pltpu.HBM) for held_in_hbm in operands))


def halves(values):
    high = values.astype(jnp.bfloat16)
    return high, (values - high.astype(jnp.float32)).astype(jnp.bfloat16)


def mix_kernel(coef_ref, cells_ref, out_ref, staged, sems):
    modes, spots, _ = cells_ref.shape
    row = lax.broadcasted_iota(jnp.int32, (modes, modes), 0)
    col = lax.broadcasted_iota(jnp.int32, (modes, modes), 1)
    mixing = jnp.where(row <= col, coef_ref[...], 0.0) + jnp.where(row == col, 1.0, 0.0)
    high, low = halves(mixing.T)
    turned = jnp.concatenate(
        [jnp.concatenate([high, high], 1), jnp.concatenate([low, low], 1)], 0
    )
    cells = cells_ref.reshape(modes * spots, LANES)
    copies = []
    for group in range(spots // SUB):
        out = staged.at[group].reshape(modes * SUB, LANES)
        for spot in range(0, SUB, 2):
            first = SUB * group + spot
            high, low = halves(jnp.concatenate(
                [cells[pl.ds(first + i, modes, stride=spots), :] for i in (0, 1)], 1
            ))
            mixed = jnp.dot(
                turned, jnp.concatenate([high, low], 0), preferred_element_type=jnp.float32
            )
            mixed = mixed[:modes] + mixed[modes:]
            for i in (0, 1):
                out[pl.ds(spot + i, modes, stride=SUB), :] = mixed[:, LANES * i:LANES * (i + 1)]
        copies.append(pltpu.make_async_copy(
            staged.at[group], out_ref.at[:, pl.ds(SUB * group, SUB)], sems.at[group]
        ))
        copies[-1].start()
    for copy in copies:
        copy.wait()


def mix(coefficients, cells):
    modes, spots, _ = cells.shape
    return pl.pallas_call(
        mix_kernel,
        out_shape=jax.ShapeDtypeStruct(cells.shape, jnp.float32),
        in_specs=[pl.BlockSpec(memory_space=pltpu.VMEM)] * 2,
        out_specs=pl.BlockSpec(memory_space=pltpu.HBM),
        scratch_shapes=[
            pltpu.VMEM((spots // SUB, modes, SUB, LANES), jnp.float32),
            pltpu.SemaphoreType.DMA((spots // SUB,)),
        ],
        compiler_params=pltpu.CompilerParams(vmem_limit_bytes=8 << 20),
    )(coefficients, cells)


def on_device_whole(tangents, checkpoints, owner_order, land_mask, coefficients):
    fields, rows = tangents.shape[1:3]
    placed = step_modes(owner_order, checkpoints, land_mask, tangents)
    mixed = mix(coefficients, placed.reshape(coefficients.shape[0], fields * rows, LANES))
    return mixed.reshape(coefficients.shape[0], fields, rows, LANES)


def on_device(tangents, checkpoints, owner_order, land_mask, coefficients):
    strips = lax.axis_size("rows")
    held, _, rows, columns = tangents.shape
    fits = (
        held % strips == 0 and strips % 2 == 0 and lax.axis_size("mode") % 2 == 0
        and lax.axis_size("mode") > 2 and rows == SUB and checkpoints.shape[-1] == LANES and strips <= 8
        and coefficients.shape[0] % LANES == 0
    )
    chosen = on_device_whole if fits else on_device_general
    return chosen(tangents, checkpoints, owner_order, land_mask, coefficients)


def solution(mesh):
    placed = (
        P("mode", None, "rows", None),
        P(None, None, "rows", "mode"),
        P(),
        P("rows", None),
        P(),
    )
    return jax.shard_map(
        on_device,
        mesh=mesh,
        in_specs=placed,
        out_specs=P(None, None, "rows", "mode"),
        check_vma=False,
    )
```

```python
import functools

import jax
import jax.numpy as jnp
from jax import lax
from jax.experimental import pallas as pl
from jax.experimental.pallas import tpu as pltpu
from jax.sharding import PartitionSpec as P

mean_depth = 1.0
gravity = 1.0
coriolis = 0.5
time_step = 0.5


def padded(cells, sides, width):
    for axis, dim in sides:
        count = lax.axis_size(axis)
        ends = count - 1
        head = lax.slice_in_dim(cells, 0, width, axis=dim)
        tail = lax.slice_in_dim(cells, cells.shape[dim] - width, cells.shape[dim], axis=dim)
        cells = jnp.concatenate(
            [
                lax.ppermute(tail, axis, [(i, (i + 1) % count) for i in range(ends)]),
                cells,
                lax.ppermute(head, axis, [((i + 1) % count, i) for i in range(ends)]),
            ],
            axis=dim,
        )
    return cells


def deriv_x(values):
    return 0.5 * (jnp.roll(values, -1, -1) - jnp.roll(values, 1, -1))


def deriv_y(values):
    return 0.5 * (values[..., 2:, :] - values[..., :-2, :])


def interior(values):
    return values[..., 1:-1, :]


def tendency(base_flow, current):
    depth_total = mean_depth + base_flow[0]
    flow_u = base_flow[1]
    flow_v = base_flow[2]
    height = current[:, 0]
    zonal = current[:, 1]
    meridional = current[:, 2]
    flux_x = depth_total * zonal + height * flow_u
    flux_y = depth_total * meridional + height * flow_v
    height_rate = -(interior(deriv_x(flux_x)) + deriv_y(flux_y))
    zonal_mid = interior(zonal)
    merid_mid = interior(meridional)
    flow_umid = interior(flow_u)
    flow_vmid = interior(flow_v)
    zonal_rate = (
        -(
            flow_umid * interior(deriv_x(zonal))
            + zonal_mid * interior(deriv_x(flow_u))
            + flow_vmid * deriv_y(zonal)
            + merid_mid * deriv_y(flow_u)
        )
        + coriolis * merid_mid
        - gravity * interior(deriv_x(height))
    )
    merid_rate = (
        -(
            flow_umid * interior(deriv_x(meridional))
            + zonal_mid * interior(deriv_x(flow_v))
            + flow_vmid * deriv_y(meridional)
            + merid_mid * deriv_y(flow_v)
        )
        - coriolis * zonal_mid
        - gravity * deriv_y(height)
    )
    return jnp.stack([height_rate, zonal_rate, merid_rate], 1)


def step_wide(base_wide, state_wide, wet_wide):
    slope_one = tendency(base_wide, state_wide)
    middle = wet_wide[1:-1] * (state_wide[:, :, 1:-1] + time_step * slope_one)
    slope_two = tendency(base_wide[:, 1:-1], middle)
    return wet_wide[2:-2] * (
        state_wide[:, :, 2:-2] + 0.5 * time_step * (slope_one[:, :, 1:-1] + slope_two)
    )


def on_device_general(tangents, checkpoints, owner_order, land_mask, coefficients):
    wet_mask = land_mask.astype(jnp.float32)
    current = wet_mask * tangents
    depth = 2
    flows_wide, wet_stack = (
        padded(checkpoints, (("rows", 2),), depth),
        padded(wet_mask[None, None], (("rows", 2),), depth),
    )
    wet_wide = wet_stack[0, 0]

    def fetch_flow(step_index):
        held_tile = lax.dynamic_index_in_dim(flows_wide, owner_order[step_index], 0, keepdims=False)
        return lax.all_gather(held_tile, "mode", axis=2, tiled=True)

    total_steps = owner_order.shape[0]

    def advance(step_index, current):
        widened = padded(current, (("rows", 2),), 2)
        return step_wide(fetch_flow(step_index), widened, wet_wide)

    final = lax.fori_loop(0, total_steps, advance, current)
    mixing = jnp.eye(coefficients.shape[0], dtype=jnp.float32) + jnp.triu(coefficients)
    cell_block = lax.all_to_all(final, "mode", split_axis=3, concat_axis=0, tiled=True)
    flattened = cell_block.reshape(cell_block.shape[0], -1)
    mixed = jnp.dot(
        mixing.T, flattened, precision=lax.Precision.HIGHEST, preferred_element_type=jnp.float32
    )
    return mixed.reshape(cell_block.shape)


LANES = 128
SUB = 8
COEFS = 7


def tile_shift(values, lane, ahead):
    tiles = values.shape[0]
    if ahead:
        rolled = pltpu.roll(values, LANES - 1, 2)
        beside = jnp.concatenate([rolled[1:], rolled[:1]], axis=0) if tiles > 1 else rolled
        return jnp.where(lane == LANES - 1, beside, rolled)
    rolled = pltpu.roll(values, 1, 2)
    beside = jnp.concatenate([rolled[-1:], rolled[:-1]], axis=0) if tiles > 1 else rolled
    return jnp.where(lane == 0, beside, rolled)


def diff_x(values, lane):
    return tile_shift(values, lane, True) - tile_shift(values, lane, False)


def zero_pads(ref, strips):
    lead = ref.shape[:-2]
    edge = jnp.zeros(lead + (SUB, LANES), jnp.float32)
    ref[..., pl.ds(0, SUB), :] = edge
    ref[..., pl.ds(SUB * (strips + 1), SUB), :] = edge


def band(strip, shift=0):
    return pl.ds(SUB * (strip + 1) + shift, SUB)


def build_coefs(order, base_ref, coef, flow_pad, strips, steps, lane):
    zero_pads(flow_pad, strips)

    def one(step, carry):
        first = 3 * order[step]
        for strip in range(strips):
            coef[step, 0, :, pl.ds(SUB * strip, SUB), :] = 0.0625 * (
                mean_depth + base_ref[:, strip, first]
            )
            flow_pad[0, :, band(strip), :] = 0.25 * base_ref[:, strip, first + 1]
            flow_pad[1, :, band(strip), :] = 0.25 * base_ref[:, strip, first + 2]
        for strip in range(strips):
            rows = pl.ds(SUB * strip, SUB)
            flow_u = flow_pad[0, :, band(strip), :]
            flow_v = flow_pad[1, :, band(strip), :]
            coef[step, 1, :, rows, :] = flow_u
            coef[step, 2, :, rows, :] = flow_v
            coef[step, 3, :, rows, :] = diff_x(flow_u, lane)
            coef[step, 4, :, rows, :] = 0.25 - (
                flow_pad[0, :, band(strip, 1), :] - flow_pad[0, :, band(strip, -1), :]
            )
            coef[step, 5, :, rows, :] = 0.25 + diff_x(flow_v, lane)
            coef[step, 6, :, rows, :] = (
                flow_pad[1, :, band(strip, 1), :] - flow_pad[1, :, band(strip, -1), :]
            )
        return carry

    lax.fori_loop(0, steps, one, 0)


def store_flux(source, flux, coef, step, strip):
    rows = pl.ds(SUB * strip, SUB)
    flux[:, band(strip), :] = (
        coef[step, 0, :, rows, :] * source[2, :, band(strip), :]
        + coef[step, 2, :, rows, :] * source[0, :, band(strip), :]
    )


def scaled_rates(source, flux, coef, step, strip, lane):
    rows = pl.ds(SUB * strip, SUB)
    here, above, below = band(strip), band(strip, 1), band(strip, -1)
    height, zonal, merid = source[0, :, here, :], source[1, :, here, :], source[2, :, here, :]
    depth, flow_u, flow_v, du_dx, turn_v, turn_u, dv_dy = (
        coef[step, i, :, rows, :] for i in range(COEFS)
    )
    flux_x = depth * zonal + flow_u * height
    rate_h = diff_x(flux_x, lane) + (flux[:, above, :] - flux[:, below, :])
    rate_u = turn_v * merid - (
        flow_u * diff_x(zonal, lane)
        + du_dx * zonal
        + flow_v * (source[1, :, above, :] - source[1, :, below, :])
        + diff_x(height, lane)
    )
    rate_v = (
        flow_u * diff_x(merid, lane)
        + turn_u * zonal
        + flow_v * (source[2, :, above, :] - source[2, :, below, :])
        + dv_dy * merid
        + (source[0, :, above, :] - source[0, :, below, :])
    )
    return (height, zonal, merid), (-rate_h, rate_u, -rate_v)


def run_steps(state, middle, flux, coef, wet, strips, steps, lane):
    def one(step, carry):
        for strip in range(strips):
            store_flux(state, flux, coef, step, strip)
        for strip in range(strips):
            held, rates = scaled_rates(state, flux, coef, step, strip, lane)
            water = wet[:, pl.ds(SUB * strip, SUB), :]
            for f in range(3):
                middle[f, :, band(strip), :] = water * (held[f] + rates[f])
        for strip in range(strips):
            store_flux(middle, flux, coef, step, strip)
        for strip in range(strips):
            held, rates = scaled_rates(middle, flux, coef, step, strip, lane)
            water = wet[:, pl.ds(SUB * strip, SUB), :]
            for f in range(3):
                state[f, :, band(strip), :] = state[f, :, band(strip), :] + water * (
                    held[f] + rates[f]
                )
        return carry

    lax.fori_loop(0, steps, one, 0)


def halves(values):
    high = values.astype(jnp.bfloat16)
    return high, (values - high.astype(jnp.float32)).astype(jnp.bfloat16)


def turned_mixing(coefficients):
    modes = coefficients.shape[0]
    row = lax.broadcasted_iota(jnp.int32, (modes, modes), 0)
    col = lax.broadcasted_iota(jnp.int32, (modes, modes), 1)
    mixing = jnp.where(row <= col, coefficients, 0.0) + jnp.where(row == col, 1.0, 0.0)
    high, low = halves(mixing.T)
    return jnp.concatenate(
        [jnp.concatenate([high, high], 1), jnp.concatenate([low, low], 1)], 0
    )


def mix_rows(turned_ref, cells_ref, group, out_ref):
    modes, spots, _ = cells_ref.shape
    cells = cells_ref.reshape(modes * spots, LANES)
    out = out_ref.reshape(modes * SUB, LANES)
    turned = turned_ref[...]
    for spot in range(0, SUB, 2):
        first = SUB * group + spot
        high, low = halves(jnp.concatenate(
            [cells[pl.ds(first + i, modes, stride=spots), :] for i in (0, 1)], 1
        ))
        mixed = jnp.dot(
            turned, jnp.concatenate([high, low], 0), preferred_element_type=jnp.float32
        )
        mixed = mixed[:modes] + mixed[modes:]
        for i in (0, 1):
            out[pl.ds(spot + i, modes, stride=SUB), :] = mixed[:, LANES * i:LANES * (i + 1)]


def steps_kernel(strips, tiles, steps, kept, order_ref, base_ref, land_ref, tan_ref, mix_ref,
                 turned_ref, out_ref, base_all, whole, mixing, leaving, coef, wet, state, middle, flux, flow_pad,
                 z_send, z_recv, x_send, x_recv, p_send, p_recv,
                 in_send, in_recv, out_send, out_recv, line, plane, half_in, cross,
                 land, order, fetch):
    m = lax.axis_index("mode")
    r = lax.axis_index("rows")
    everyone = tiles * strips
    me = m * strips + r
    chips = tiles // 2
    pairs = 2 * (m // 2)
    core = m - pairs
    partner = pairs + 1 - core
    mask_at = 3 * steps
    lane = lax.broadcasted_iota(jnp.int32, (tiles, SUB, LANES), 2)

    def other_chip(j):
        return lax.rem(m + 2 * j, tiles)

    def send(source, target, sent, received, mode, row):
        pltpu.make_async_remote_copy(
            src_ref=source, dst_ref=target, send_sem=sent, recv_sem=received,
            device_id=(mode, row), device_id_type=pl.DeviceIdType.MESH,
        ).start()

    def beside(step):
        chip, target, bit = m // 2, 0, 1
        if chips & (chips - 1):
            return lax.rem(chip + step, chips)
        while bit < chips:
            target = target + bit * ((chip // bit + step // bit) % 2)
            bit = 2 * bit
        return target

    farthest_first = []
    for step in reversed(range(chips)):
        chip_there = beside(step)
        farthest_first += [2 * chip_there + 1 - core, 2 * chip_there + core]

    def drain(ref, sem):
        pltpu.make_async_copy(ref, ref, sem).wait()

    barrier = pltpu.get_barrier_semaphore()
    half = strips // 2
    upper = r >= half
    at_end = jnp.logical_or(r == 0, r == strips - 1)
    at_mid = jnp.logical_or(r == half - 1, r == half)
    not_end, not_mid = jnp.logical_not(at_end), jnp.logical_not(at_mid)
    inner = jnp.where(upper, r - 1, r + 1)
    outer = jnp.where(upper, r + 1, r - 1)

    def signal(sem, mode, row):
        pl.semaphore_signal(
            sem, inc=1, device_id=(mode, row), device_id_type=pl.DeviceIdType.MESH
        )

    def signal_plane(sem):
        for j in range(1, tiles):
            signal(sem, lax.rem(m + j, tiles), r)

    def sibling(i):
        return jnp.where(upper, half + lax.rem(r + i, half), lax.rem(r + i, half))

    def opposite(i):
        return jnp.where(upper, half - 1 - i, half + i)

    @pl.when(at_mid)
    def _():
        signal(barrier, m, inner)

    @pl.when(jnp.logical_and(at_mid, not_end))
    def _():
        signal(barrier, m, outer)

    @pl.when(at_end)
    def _():
        signal_plane(barrier)

    own = base_all.at[m, r]
    tile_of_land = land_ref.at[:, pl.ds(pl.multiple_of(m * LANES, LANES), LANES)]
    fetch_base = pltpu.make_async_copy(base_ref, own.at[pl.ds(0, mask_at)], fetch.at[0])
    fetch_land = pltpu.make_async_copy(tile_of_land, land, fetch.at[1])
    fetch_order = pltpu.make_async_copy(order_ref, order, fetch.at[2])
    fetch_mixing = pltpu.make_async_copy(mix_ref, mixing, fetch.at[3])
    fetch_land.start()
    fetch_base.start()
    fetch_order.start()
    fetch_mixing.start()

    @pl.when(at_end)
    def _():
        pl.semaphore_wait(barrier, tiles)

    @pl.when(not_end)
    def _():
        pl.semaphore_wait(barrier, 1)

    if half > 2:

        @pl.when(jnp.logical_and(not_end, not_mid))
        def _():
            signal(barrier, m, outer)

    def send_in(k, q):
        send(tan_ref.at[q * kept + k], whole.at[k, r], in_send, in_recv.at[k], m, q)

    def pass_up(q):
        strip = base_all.at[m, q]
        send(strip, strip, z_send.at[0, q], z_recv.at[q], m, r + 1)

    def pass_down(q):
        strip = base_all.at[m, q]
        send(strip, strip, z_send.at[1, q], z_recv.at[q], m, r - 1)

    def spread(q):
        strip = base_all.at[m, q]
        for j in range(1, chips):
            send(strip, strip, x_send, x_recv.at[m], other_chip(j), r)

    def relay(q):

        @pl.when(jnp.logical_and(q < r, r < strips - 1))
        def _():
            pass_up(q)

        @pl.when(jnp.logical_and(q > r, r > 0))
        def _():
            pass_down(q)

        spread(q)

    def take_below(j):

        @pl.when(r >= j)
        def _():
            drain(base_all.at[m, r - j], z_recv.at[r - j])
            relay(r - j)

    def take_above(j):

        @pl.when(r + j < strips)
        def _():
            drain(base_all.at[m, r + j], z_recv.at[r + j])
            relay(r + j)

    def hop(j):
        @pl.when(upper)
        def _():
            take_above(j)

        take_below(j)

        @pl.when(jnp.logical_not(upper))
        def _():
            take_above(j)

    def send_near(k):
        send_in(k, opposite(0))

    def send_far(k):
        for i in range(1, half):
            send_in(k, opposite(i))

    def send_half(k):
        for i in range(1, half):
            send_in(k, sibling(i))

    modes = range(kept)

    @pl.when(at_mid)
    def _():
        send_near(0)

    fetch_land.wait()
    own[mask_at] = land[...].astype(jnp.float32)
    fetch_base.wait()
    fetch_order.wait()

    @pl.when(upper)
    def _():
        pass_down(r)

    @pl.when(jnp.logical_not(upper))
    def _():
        pass_up(r)

    @pl.when(not_mid)
    def _():
        signal(line, m, inner)

    @pl.when(at_end)
    def _():
        signal_plane(plane)
        spread(r)

    @pl.when(not_end)
    def _():
        pl.semaphore_wait(line, 1)

        @pl.when(upper)
        def _():
            pass_up(r)

        @pl.when(jnp.logical_not(upper))
        def _():
            pass_down(r)

    @pl.when(at_mid)
    def _():
        for k in modes[1:2]:
            send_near(k)

    @pl.when(at_end)
    def _():
        pl.semaphore_wait(plane, tiles - 1)
        for i in range(1, half):
            signal(half_in, m, sibling(i))

    @pl.when(not_end)
    def _():
        pl.semaphore_wait(half_in, 1)
        spread(r)

    @pl.when(at_mid)
    def _():
        signal(cross, m, inner)

    hop(1)
    send_half(0)

    @pl.when(at_mid)
    def _():
        pl.semaphore_wait(cross, 1)
        for i in range(1, half):
            signal(cross, m, sibling(i))
        for k in modes[2:]:
            send_near(k)

    for j in range(2, strips):
        hop(j)
        if j == 2:

            @pl.when(not_mid)
            def _():
                pl.semaphore_wait(cross, 1)
                send_near(0)

    def send_rest(far, near, beside):
        for k in far:
            send_far(k)

        @pl.when(not_mid)
        def _():
            for k in near:
                send_near(k)

        for k in beside:
            send_half(k)

    send_rest(modes[:1], modes[1:2], modes[1:2])

    @pl.when(at_mid)
    def _():
        for k in modes[1:2]:
            send_far(k)

    for k in range(kept):
        pltpu.make_async_copy(tan_ref.at[r * kept + k], whole.at[k, r], in_recv.at[k]).start()
    send(base_all.at[m], base_all.at[m], p_send, p_recv, partner, r)
    for ref in (state, middle, flux):
        zero_pads(ref, strips)
    for j in range(1, chips):
        tile = other_chip(j)
        drain(base_all.at[tile], x_recv.at[tile])
        send(base_all.at[tile], base_all.at[tile], p_send, p_recv, partner, r)
    @pl.when(not_mid)
    def _():
        for k in modes[1:2]:
            send_far(k)

    send_rest((), modes[2:3], modes[2:3])
    drain(base_all.at[pl.ds(0, chips)], p_recv)
    send_rest(modes[2:], modes[3:], modes[3:])

    for strip in range(strips):
        wet[:, pl.ds(SUB * strip, SUB), :] = base_all[:, strip, mask_at]
    build_coefs(order, base_all, coef, flow_pad, strips, steps, lane)

    def one_mode(k, carry):
        drain(whole.at[k], in_recv.at[k])
        for f, scale in enumerate((0.25, 1.0, 1.0)):
            for strip in range(strips):
                for t in range(tiles):
                    state[f, t, band(strip), :] = (
                        scale * wet[t, pl.ds(SUB * strip, SUB), :]
                    ) * whole[k, strip, f, :, pl.ds(LANES * t, LANES)]
        run_steps(state, middle, flux, coef, wet, strips, steps, lane)
        down = 0.5 ** steps
        for f, scale in enumerate((4.0 * down, down, down)):
            for strip in range(strips):
                for t in range(tiles):
                    leaving[k, t * strips + strip, f] = scale * state[f, t, band(strip), :]

        def post_row(row):
            def to(mode):
                send(leaving.at[k, mode * strips + row], out_ref.at[me, k], out_send, out_recv,
                     mode, row)

            for lead in (0, 1):

                @pl.when(jnp.logical_and(row == 0, jnp.logical_or(row != r, m != lead)))
                def _():
                    to(lead)

            for mode in farthest_first:
                skip = jnp.logical_or(
                    jnp.logical_and(row == r, mode == m), jnp.logical_and(row == 0, mode < 2)
                )

                @pl.when(jnp.logical_not(skip))
                def _():
                    to(mode)

        for i in range(half):
            post_row(opposite(half - 1 - i))
        for i in range(1, half):
            post_row(sibling(i))
        post_row(r)
        pltpu.make_async_copy(leaving.at[k, me], out_ref.at[me, k], out_recv).start()
        return carry

    lax.fori_loop(0, kept, one_mode, 0)
    fetch_mixing.wait()
    turned_ref[...] = turned_mixing(mixing[...])
    for q in range(strips):

        @pl.when(jnp.logical_and(q <= r, r < strips - 1))
        def _():
            drain(base_all.at[m, q], z_send.at[0, q])

        @pl.when(jnp.logical_and(q >= r, r > 0))
        def _():
            drain(base_all.at[m, q], z_send.at[1, q])

    drain(base_all.at[pl.ds(0, chips - 1)], x_send)
    drain(base_all.at[pl.ds(0, chips)], p_send)
    drain(whole.at[:, pl.ds(0, strips - 1)], in_send)
    drain(leaving.at[:, pl.ds(0, everyone - 1)], out_send)
    drain(out_ref, out_recv)


def step_modes(order, base, land, tangents, coefficients):
    strips, tiles = lax.axis_size("rows"), lax.axis_size("mode")
    held, fields, rows, columns = tangents.shape
    steps = base.shape[0]
    kept = held // strips
    everyone = tiles * strips
    modes = everyone * kept
    tall = SUB * (strips + 2)
    hbm, vmem = (pl.BlockSpec(memory_space=space) for space in (pltpu.HBM, pltpu.VMEM))
    operands = (order, base.reshape(steps * fields, rows, LANES), land, tangents, coefficients)
    dma, regular = pltpu.SemaphoreType.DMA, pltpu.SemaphoreType.REGULAR
    return pl.pallas_call(
        functools.partial(steps_kernel, strips, tiles, steps, kept),
        out_shape=(
            jax.ShapeDtypeStruct((2 * modes, 2 * modes), jnp.bfloat16),
            jax.ShapeDtypeStruct((everyone, kept, fields, rows, LANES), jnp.float32),
        ),
        in_specs=[hbm] * 5,
        out_specs=(vmem, pl.BlockSpec(memory_space=pl.ANY)),
        scratch_shapes=[
            pltpu.VMEM((tiles, strips, steps * fields + 1, rows, LANES), jnp.float32),
            pltpu.VMEM((kept, strips, fields, rows, columns), jnp.float32),
            pltpu.VMEM((modes, modes), jnp.float32),
            pltpu.VMEM((kept, everyone, fields, rows, LANES), jnp.float32),
            pltpu.VMEM((steps, COEFS, tiles, SUB * strips, LANES), jnp.float32),
            pltpu.VMEM((tiles, SUB * strips, LANES), jnp.float32),
            pltpu.VMEM((3, tiles, tall, LANES), jnp.float32),
            pltpu.VMEM((3, tiles, tall, LANES), jnp.float32),
            pltpu.VMEM((tiles, tall, LANES), jnp.float32),
            pltpu.VMEM((2, tiles, tall, LANES), jnp.float32),
            dma((2, strips)), dma((strips,)), dma, dma((tiles,)), dma, dma,
            dma, dma((kept,)), dma, dma,
            regular, regular, regular, regular,
            pltpu.VMEM((rows, LANES), jnp.int32), pltpu.SMEM((steps,), jnp.int32), dma((4,)),
        ],
        compiler_params=pltpu.CompilerParams(
            collective_id=0, has_side_effects=True, vmem_limit_bytes=32 << 20
        ),
    )(*(pltpu.with_memory_space_constraint(held_in_hbm, pltpu.HBM) for held_in_hbm in operands))


def mix_kernel(turned_ref, cells_ref, out_ref, staged, sems):
    copies = []
    for group in range(staged.shape[0]):
        mix_rows(turned_ref, cells_ref, group, staged.at[group])
        copies.append(pltpu.make_async_copy(
            staged.at[group], out_ref.at[:, pl.ds(SUB * group, SUB)], sems.at[group]
        ))
        copies[-1].start()
    for copy in copies:
        copy.wait()


def mix(turned, cells):
    modes, spots, _ = cells.shape
    return pl.pallas_call(
        mix_kernel,
        out_shape=jax.ShapeDtypeStruct(cells.shape, jnp.float32),
        in_specs=[pl.BlockSpec(memory_space=pltpu.VMEM)] * 2,
        out_specs=pl.BlockSpec(memory_space=pltpu.HBM),
        scratch_shapes=[
            pltpu.VMEM((spots // SUB, modes, SUB, LANES), jnp.float32),
            pltpu.SemaphoreType.DMA((spots // SUB,)),
        ],
        compiler_params=pltpu.CompilerParams(vmem_limit_bytes=8 << 20),
    )(turned, cells)


def on_device_whole(tangents, checkpoints, owner_order, land_mask, coefficients):
    fields, rows = tangents.shape[1:3]
    turned, placed = step_modes(owner_order, checkpoints, land_mask, tangents, coefficients)
    whole = mix(turned, placed.reshape(-1, fields * rows, LANES))
    return whole.reshape(-1, fields, rows, LANES)


def on_device(tangents, checkpoints, owner_order, land_mask, coefficients):
    strips = lax.axis_size("rows")
    held, _, rows, columns = tangents.shape
    fits = (
        held % strips == 0 and strips % 2 == 0 and lax.axis_size("mode") % 2 == 0
        and lax.axis_size("mode") > 2 and rows == SUB and checkpoints.shape[-1] == LANES and strips <= 8
        and coefficients.shape[0] == held * lax.axis_size("mode")
        and coefficients.shape[0] % LANES == 0
    )
    chosen = on_device_whole if fits else on_device_general
    return chosen(tangents, checkpoints, owner_order, land_mask, coefficients)


def solution(mesh):
    placed = (
        P("mode", None, "rows", None),
        P(None, None, "rows", "mode"),
        P(),
        P("rows", None),
        P(),
    )
    return jax.shard_map(
        on_device,
        mesh=mesh,
        in_specs=placed,
        out_specs=P(None, None, "rows", "mode"),
        check_vma=False,
    )
```

```python
import functools

import jax
import jax.numpy as jnp
from jax import lax
from jax.experimental import pallas as pl
from jax.experimental.pallas import tpu as pltpu
from jax.sharding import PartitionSpec as P

mean_depth = 1.0
gravity = 1.0
coriolis = 0.5
time_step = 0.5


def padded(cells, sides, width):
    for axis, dim in sides:
        count = lax.axis_size(axis)
        ends = count - 1
        head = lax.slice_in_dim(cells, 0, width, axis=dim)
        tail = lax.slice_in_dim(cells, cells.shape[dim] - width, cells.shape[dim], axis=dim)
        cells = jnp.concatenate(
            [
                lax.ppermute(tail, axis, [(i, (i + 1) % count) for i in range(ends)]),
                cells,
                lax.ppermute(head, axis, [((i + 1) % count, i) for i in range(ends)]),
            ],
            axis=dim,
        )
    return cells


def deriv_x(values):
    return 0.5 * (jnp.roll(values, -1, -1) - jnp.roll(values, 1, -1))


def deriv_y(values):
    return 0.5 * (values[..., 2:, :] - values[..., :-2, :])


def interior(values):
    return values[..., 1:-1, :]


def tendency(base_flow, current):
    depth_total = mean_depth + base_flow[0]
    flow_u = base_flow[1]
    flow_v = base_flow[2]
    height = current[:, 0]
    zonal = current[:, 1]
    meridional = current[:, 2]
    flux_x = depth_total * zonal + height * flow_u
    flux_y = depth_total * meridional + height * flow_v
    height_rate = -(interior(deriv_x(flux_x)) + deriv_y(flux_y))
    zonal_mid = interior(zonal)
    merid_mid = interior(meridional)
    flow_umid = interior(flow_u)
    flow_vmid = interior(flow_v)
    zonal_rate = (
        -(
            flow_umid * interior(deriv_x(zonal))
            + zonal_mid * interior(deriv_x(flow_u))
            + flow_vmid * deriv_y(zonal)
            + merid_mid * deriv_y(flow_u)
        )
        + coriolis * merid_mid
        - gravity * interior(deriv_x(height))
    )
    merid_rate = (
        -(
            flow_umid * interior(deriv_x(meridional))
            + zonal_mid * interior(deriv_x(flow_v))
            + flow_vmid * deriv_y(meridional)
            + merid_mid * deriv_y(flow_v)
        )
        - coriolis * zonal_mid
        - gravity * deriv_y(height)
    )
    return jnp.stack([height_rate, zonal_rate, merid_rate], 1)


def step_wide(base_wide, state_wide, wet_wide):
    slope_one = tendency(base_wide, state_wide)
    middle = wet_wide[1:-1] * (state_wide[:, :, 1:-1] + time_step * slope_one)
    slope_two = tendency(base_wide[:, 1:-1], middle)
    return wet_wide[2:-2] * (
        state_wide[:, :, 2:-2] + 0.5 * time_step * (slope_one[:, :, 1:-1] + slope_two)
    )


def on_device_general(tangents, checkpoints, owner_order, land_mask, coefficients):
    wet_mask = land_mask.astype(jnp.float32)
    current = wet_mask * tangents
    depth = 2
    flows_wide, wet_stack = (
        padded(checkpoints, (("rows", 2),), depth),
        padded(wet_mask[None, None], (("rows", 2),), depth),
    )
    wet_wide = wet_stack[0, 0]

    def fetch_flow(step_index):
        held_tile = lax.dynamic_index_in_dim(flows_wide, owner_order[step_index], 0, keepdims=False)
        return lax.all_gather(held_tile, "mode", axis=2, tiled=True)

    total_steps = owner_order.shape[0]

    def advance(step_index, current):
        widened = padded(current, (("rows", 2),), 2)
        return step_wide(fetch_flow(step_index), widened, wet_wide)

    final = lax.fori_loop(0, total_steps, advance, current)
    mixing = jnp.eye(coefficients.shape[0], dtype=jnp.float32) + jnp.triu(coefficients)
    cell_block = lax.all_to_all(final, "mode", split_axis=3, concat_axis=0, tiled=True)
    flattened = cell_block.reshape(cell_block.shape[0], -1)
    mixed = jnp.dot(
        mixing.T, flattened, precision=lax.Precision.HIGHEST, preferred_element_type=jnp.float32
    )
    return mixed.reshape(cell_block.shape)


LANES = 128
SUB = 8
COEFS = 7


def tile_shift(values, lane, ahead):
    tiles = values.shape[0]
    if ahead:
        rolled = pltpu.roll(values, LANES - 1, 2)
        beside = jnp.concatenate([rolled[1:], rolled[:1]], axis=0) if tiles > 1 else rolled
        return jnp.where(lane == LANES - 1, beside, rolled)
    rolled = pltpu.roll(values, 1, 2)
    beside = jnp.concatenate([rolled[-1:], rolled[:-1]], axis=0) if tiles > 1 else rolled
    return jnp.where(lane == 0, beside, rolled)


def diff_x(values, lane):
    return tile_shift(values, lane, True) - tile_shift(values, lane, False)


def zero_pads(ref, strips):
    lead = ref.shape[:-2]
    edge = jnp.zeros(lead + (SUB, LANES), jnp.float32)
    ref[..., pl.ds(0, SUB), :] = edge
    ref[..., pl.ds(SUB * (strips + 1), SUB), :] = edge


def band(strip, shift=0):
    return pl.ds(SUB * (strip + 1) + shift, SUB)


def build_coefs(order, base_ref, coef, flow_pad, strips, steps, lane):
    zero_pads(flow_pad, strips)

    def one(step, carry):
        first = 3 * order[step]
        for strip in range(strips):
            coef[step, 0, :, pl.ds(SUB * strip, SUB), :] = 0.0625 * (
                mean_depth + base_ref[:, strip, first]
            )
            flow_pad[0, :, band(strip), :] = 0.25 * base_ref[:, strip, first + 1]
            flow_pad[1, :, band(strip), :] = 0.25 * base_ref[:, strip, first + 2]
        for strip in range(strips):
            rows = pl.ds(SUB * strip, SUB)
            flow_u = flow_pad[0, :, band(strip), :]
            flow_v = flow_pad[1, :, band(strip), :]
            coef[step, 1, :, rows, :] = flow_u
            coef[step, 2, :, rows, :] = flow_v
            coef[step, 3, :, rows, :] = diff_x(flow_u, lane)
            coef[step, 4, :, rows, :] = 0.25 - (
                flow_pad[0, :, band(strip, 1), :] - flow_pad[0, :, band(strip, -1), :]
            )
            coef[step, 5, :, rows, :] = 0.25 + diff_x(flow_v, lane)
            coef[step, 6, :, rows, :] = (
                flow_pad[1, :, band(strip, 1), :] - flow_pad[1, :, band(strip, -1), :]
            )
        return carry

    lax.fori_loop(0, steps, one, 0)


def store_flux(source, flux, coef, step, strip):
    rows = pl.ds(SUB * strip, SUB)
    flux[:, band(strip), :] = (
        coef[step, 0, :, rows, :] * source[2, :, band(strip), :]
        + coef[step, 2, :, rows, :] * source[0, :, band(strip), :]
    )


def scaled_rates(source, flux, coef, step, strip, lane):
    rows = pl.ds(SUB * strip, SUB)
    here, above, below = band(strip), band(strip, 1), band(strip, -1)
    height, zonal, merid = source[0, :, here, :], source[1, :, here, :], source[2, :, here, :]
    depth, flow_u, flow_v, du_dx, turn_v, turn_u, dv_dy = (
        coef[step, i, :, rows, :] for i in range(COEFS)
    )
    flux_x = depth * zonal + flow_u * height
    rate_h = diff_x(flux_x, lane) + (flux[:, above, :] - flux[:, below, :])
    rate_u = turn_v * merid - (
        flow_u * diff_x(zonal, lane)
        + du_dx * zonal
        + flow_v * (source[1, :, above, :] - source[1, :, below, :])
        + diff_x(height, lane)
    )
    rate_v = (
        flow_u * diff_x(merid, lane)
        + turn_u * zonal
        + flow_v * (source[2, :, above, :] - source[2, :, below, :])
        + dv_dy * merid
        + (source[0, :, above, :] - source[0, :, below, :])
    )
    return (height, zonal, merid), (-rate_h, rate_u, -rate_v)


def run_steps(state, middle, flux, coef, wet, strips, steps, lane):
    def one(step, carry):
        for strip in range(strips):
            store_flux(state, flux, coef, step, strip)
        for strip in range(strips):
            held, rates = scaled_rates(state, flux, coef, step, strip, lane)
            water = wet[:, pl.ds(SUB * strip, SUB), :]
            for f in range(3):
                middle[f, :, band(strip), :] = water * (held[f] + rates[f])
        for strip in range(strips):
            store_flux(middle, flux, coef, step, strip)
        for strip in range(strips):
            held, rates = scaled_rates(middle, flux, coef, step, strip, lane)
            water = wet[:, pl.ds(SUB * strip, SUB), :]
            for f in range(3):
                state[f, :, band(strip), :] = state[f, :, band(strip), :] + water * (
                    held[f] + rates[f]
                )
        return carry

    lax.fori_loop(0, steps, one, 0)


def halves(values):
    high = values.astype(jnp.bfloat16)
    return high, (values - high.astype(jnp.float32)).astype(jnp.bfloat16)


def full_mixing(coefficients):
    modes = coefficients.shape[0]
    row = lax.broadcasted_iota(jnp.int32, (modes, modes), 0)
    col = lax.broadcasted_iota(jnp.int32, (modes, modes), 1)
    return jnp.where(row <= col, coefficients, 0.0) + jnp.where(row == col, 1.0, 0.0)


def turned_mixing(mixing):
    high, low = halves(mixing.T)
    return jnp.concatenate(
        [jnp.concatenate([high, high], 1), jnp.concatenate([low, low], 1)], 0
    )


def turned_few(mixing):
    high, low = halves(mixing.T)
    return jnp.concatenate([high, high, low, low], 1)


def mix_rows(turned_ref, cells_ref, group, out_ref):
    modes, spots, _ = cells_ref.shape
    cells = cells_ref.reshape(modes * spots, LANES)
    out = out_ref.reshape(modes * SUB, LANES)
    turned = turned_ref[...]
    for spot in range(0, SUB, 2):
        first = SUB * group + spot
        high, low = halves(jnp.concatenate(
            [cells[pl.ds(first + i, modes, stride=spots), :] for i in (0, 1)], 1
        ))
        mixed = jnp.dot(
            turned, jnp.concatenate([high, low], 0), preferred_element_type=jnp.float32
        )
        mixed = mixed[:modes] + mixed[modes:]
        for i in (0, 1):
            out[pl.ds(spot + i, modes, stride=SUB), :] = mixed[:, LANES * i:LANES * (i + 1)]


def steps_kernel(strips, tiles, steps, kept, order_ref, base_ref, land_ref, tan_ref, mix_ref,
                 few_ref, partial_ref, late_ref, cells, base_all, whole, mixing, turned, leaving, coef, wet, state, middle, flux, flow_pad,
                 z_send, z_recv, x_send, x_recv, p_send, p_recv,
                 in_send, in_recv, out_send, out_recv, late_recv, line, plane, half_in, cross,
                 land, order, fetch):
    m = lax.axis_index("mode")
    r = lax.axis_index("rows")
    everyone = tiles * strips
    me = m * strips + r
    chips = tiles // 2
    pairs = 2 * (m // 2)
    core = m - pairs
    partner = pairs + 1 - core
    mask_at = 3 * steps
    lane = lax.broadcasted_iota(jnp.int32, (tiles, SUB, LANES), 2)

    def other_chip(j):
        return lax.rem(m + 2 * j, tiles)

    def send(source, target, sent, received, mode, row):
        pltpu.make_async_remote_copy(
            src_ref=source, dst_ref=target, send_sem=sent, recv_sem=received,
            device_id=(mode, row), device_id_type=pl.DeviceIdType.MESH,
        ).start()

    def beside(step):
        chip, target, bit = m // 2, 0, 1
        if chips & (chips - 1):
            return lax.rem(chip + step, chips)
        while bit < chips:
            target = target + bit * ((chip // bit + step // bit) % 2)
            bit = 2 * bit
        return target

    farthest_first = []
    for step in reversed(range(chips)):
        chip_there = beside(step)
        farthest_first += [2 * chip_there + 1 - core, 2 * chip_there + core]

    def drain(ref, sem):
        pltpu.make_async_copy(ref, ref, sem).wait()

    barrier = pltpu.get_barrier_semaphore()
    half = strips // 2
    upper = r >= half
    at_end = jnp.logical_or(r == 0, r == strips - 1)
    at_mid = jnp.logical_or(r == half - 1, r == half)
    not_end, not_mid = jnp.logical_not(at_end), jnp.logical_not(at_mid)
    inner = jnp.where(upper, r - 1, r + 1)
    outer = jnp.where(upper, r + 1, r - 1)

    def signal(sem, mode, row):
        pl.semaphore_signal(
            sem, inc=1, device_id=(mode, row), device_id_type=pl.DeviceIdType.MESH
        )

    def signal_plane(sem):
        for j in range(1, tiles):
            signal(sem, lax.rem(m + j, tiles), r)

    def sibling(i):
        return jnp.where(upper, half + lax.rem(r + i, half), lax.rem(r + i, half))

    def opposite(i):
        return jnp.where(upper, half - 1 - i, half + i)

    @pl.when(at_mid)
    def _():
        signal(barrier, m, inner)

    @pl.when(jnp.logical_and(at_mid, not_end))
    def _():
        signal(barrier, m, outer)

    @pl.when(at_end)
    def _():
        signal_plane(barrier)

    own = base_all.at[m, r]
    tile_of_land = land_ref.at[:, pl.ds(pl.multiple_of(m * LANES, LANES), LANES)]
    fetch_base = pltpu.make_async_copy(base_ref, own.at[pl.ds(0, mask_at)], fetch.at[0])
    fetch_land = pltpu.make_async_copy(tile_of_land, land, fetch.at[1])
    fetch_order = pltpu.make_async_copy(order_ref, order, fetch.at[2])
    fetch_mixing = pltpu.make_async_copy(mix_ref, mixing, fetch.at[3])
    fetch_land.start()
    fetch_base.start()
    fetch_order.start()
    fetch_mixing.start()

    @pl.when(at_end)
    def _():
        pl.semaphore_wait(barrier, tiles)

    @pl.when(not_end)
    def _():
        pl.semaphore_wait(barrier, 1)

    if half > 2:

        @pl.when(jnp.logical_and(not_end, not_mid))
        def _():
            signal(barrier, m, outer)

    def send_in(k, q):
        send(tan_ref.at[q * kept + k], whole.at[k, r], in_send, in_recv.at[k], m, q)

    def pass_up(q):
        strip = base_all.at[m, q]
        send(strip, strip, z_send.at[0, q], z_recv.at[q], m, r + 1)

    def pass_down(q):
        strip = base_all.at[m, q]
        send(strip, strip, z_send.at[1, q], z_recv.at[q], m, r - 1)

    def spread(q):
        strip = base_all.at[m, q]
        for j in range(1, chips):
            send(strip, strip, x_send, x_recv.at[m], other_chip(j), r)

    def relay(q):

        @pl.when(jnp.logical_and(q < r, r < strips - 1))
        def _():
            pass_up(q)

        @pl.when(jnp.logical_and(q > r, r > 0))
        def _():
            pass_down(q)

        spread(q)

    def take_below(j):

        @pl.when(r >= j)
        def _():
            drain(base_all.at[m, r - j], z_recv.at[r - j])
            relay(r - j)

    def take_above(j):

        @pl.when(r + j < strips)
        def _():
            drain(base_all.at[m, r + j], z_recv.at[r + j])
            relay(r + j)

    def hop(j):
        @pl.when(upper)
        def _():
            take_above(j)

        take_below(j)

        @pl.when(jnp.logical_not(upper))
        def _():
            take_above(j)

    def send_near(k):
        send_in(k, opposite(0))

    def send_far(k):
        for i in range(1, half):
            send_in(k, opposite(i))

    def send_half(k):
        for i in range(1, half):
            send_in(k, sibling(i))

    modes = range(kept)

    @pl.when(at_mid)
    def _():
        send_near(0)

    fetch_land.wait()
    own[mask_at] = land[...].astype(jnp.float32)
    fetch_base.wait()
    fetch_order.wait()

    @pl.when(upper)
    def _():
        pass_down(r)

    @pl.when(jnp.logical_not(upper))
    def _():
        pass_up(r)

    @pl.when(not_mid)
    def _():
        signal(line, m, inner)

    @pl.when(at_end)
    def _():
        signal_plane(plane)
        spread(r)

    @pl.when(not_end)
    def _():
        pl.semaphore_wait(line, 1)

        @pl.when(upper)
        def _():
            pass_up(r)

        @pl.when(jnp.logical_not(upper))
        def _():
            pass_down(r)

    @pl.when(at_mid)
    def _():
        for k in modes[1:2]:
            send_near(k)

    @pl.when(at_end)
    def _():
        pl.semaphore_wait(plane, tiles - 1)
        for i in range(1, half):
            signal(half_in, m, sibling(i))

    @pl.when(not_end)
    def _():
        pl.semaphore_wait(half_in, 1)
        spread(r)

    @pl.when(at_mid)
    def _():
        signal(cross, m, inner)

    hop(1)
    send_half(0)

    @pl.when(at_mid)
    def _():
        pl.semaphore_wait(cross, 1)
        for i in range(1, half):
            signal(cross, m, sibling(i))
        for k in modes[2:]:
            send_near(k)

    for j in range(2, strips):
        hop(j)
        if j == 2:

            @pl.when(not_mid)
            def _():
                pl.semaphore_wait(cross, 1)
                send_near(0)

    def send_rest(far, near, beside):
        for k in far:
            send_far(k)

        @pl.when(not_mid)
        def _():
            for k in near:
                send_near(k)

        for k in beside:
            send_half(k)

    send_rest(modes[:1], modes[1:2], modes[1:2])

    @pl.when(at_mid)
    def _():
        for k in modes[1:2]:
            send_far(k)

    for k in range(kept):
        pltpu.make_async_copy(tan_ref.at[r * kept + k], whole.at[k, r], in_recv.at[k]).start()
    send(base_all.at[m], base_all.at[m], p_send, p_recv, partner, r)
    for ref in (state, middle, flux):
        zero_pads(ref, strips)
    for j in range(1, chips):
        tile = other_chip(j)
        drain(base_all.at[tile], x_recv.at[tile])
        send(base_all.at[tile], base_all.at[tile], p_send, p_recv, partner, r)
    @pl.when(not_mid)
    def _():
        for k in modes[1:2]:
            send_far(k)

    send_rest((), modes[2:3], modes[2:3])
    drain(base_all.at[pl.ds(0, chips)], p_recv)
    send_rest(modes[2:], modes[3:], modes[3:])

    for strip in range(strips):
        wet[:, pl.ds(SUB * strip, SUB), :] = base_all[:, strip, mask_at]
    build_coefs(order, base_all, coef, flow_pad, strips, steps, lane)

    final = kept - 1
    slot = lax.rem(r, half) * tiles + m

    def one_mode(k, carry, last=False):
        drain(whole.at[k], in_recv.at[k])
        for f, scale in enumerate((0.25, 1.0, 1.0)):
            for strip in range(strips):
                for t in range(tiles):
                    state[f, t, band(strip), :] = (
                        scale * wet[t, pl.ds(SUB * strip, SUB), :]
                    ) * whole[k, strip, f, :, pl.ds(LANES * t, LANES)]
        run_steps(state, middle, flux, coef, wet, strips, steps, lane)
        down = 0.5 ** steps
        for f, scale in enumerate((4.0 * down, down, down)):
            for strip in range(strips):
                for t in range(tiles):
                    leaving[k, t * strips + strip, f] = scale * state[f, t, band(strip), :]

        def post_row(row, late=False):
            def to(mode):
                target, received = (
                    (late_ref.at[slot], late_recv) if late else (cells.at[me, k], out_recv)
                )
                send(leaving.at[k, mode * strips + row], target, out_send, received, mode, row)

            for lead in (0, 1):

                @pl.when(jnp.logical_and(row == 0, jnp.logical_or(row != r, m != lead)))
                def _():
                    to(lead)

            for mode in farthest_first:
                skip = jnp.logical_or(
                    jnp.logical_and(row == r, mode == m), jnp.logical_and(row == 0, mode < 2)
                )

                @pl.when(jnp.logical_not(skip))
                def _():
                    to(mode)

        for i in range(half):
            post_row(opposite(half - 1 - i), last)
        for i in range(1, half):
            post_row(sibling(i))
        post_row(r)
        pltpu.make_async_copy(leaving.at[k, me], cells.at[me, k], out_recv).start()
        return carry

    lax.fori_loop(0, final, one_mode, 0)
    one_mode(final, 0, last=True)

    there = jnp.where(upper, 0, half)
    fetch_mixing.wait()
    mixing[...] = full_mixing(mixing[...])
    turned[...] = turned_mixing(mixing[...])
    pace = strips * kept

    def few_rows(first):
        return jnp.concatenate(
            [mixing[pl.ds((first + i) * kept + final, tiles, stride=pace), :] for i in range(half)], 0
        )

    few_ref[...] = turned_few(jnp.where(upper, few_rows(0), few_rows(half)))
    for mode in range(tiles):
        for i in range(half):
            cells[mode * strips + there + i, final] = jnp.zeros(cells.shape[2:], jnp.float32)
    early = everyone * final + everyone // 2
    drain(cells.reshape((everyone * kept,) + cells.shape[2:]).at[pl.ds(0, early)], out_recv)
    spots = cells.shape[2] * SUB
    for group in range(cells.shape[2]):
        mix_rows(turned, cells.reshape(everyone * kept, spots, LANES), group, partial_ref.at[group])

    for q in range(strips):

        @pl.when(jnp.logical_and(q <= r, r < strips - 1))
        def _():
            drain(base_all.at[m, q], z_send.at[0, q])

        @pl.when(jnp.logical_and(q >= r, r > 0))
        def _():
            drain(base_all.at[m, q], z_send.at[1, q])

    drain(base_all.at[pl.ds(0, chips - 1)], x_send)
    drain(base_all.at[pl.ds(0, chips)], p_send)
    drain(whole.at[:, pl.ds(0, strips - 1)], in_send)
    drain(leaving.at[:, pl.ds(0, everyone - 1)], out_send)
    drain(late_ref, late_recv)


def step_modes(order, base, land, tangents, coefficients):
    strips, tiles = lax.axis_size("rows"), lax.axis_size("mode")
    held, fields, rows, columns = tangents.shape
    steps = base.shape[0]
    kept = held // strips
    everyone = tiles * strips
    modes, late = everyone * kept, everyone // 2
    tall = SUB * (strips + 2)
    hbm, vmem = (pl.BlockSpec(memory_space=space) for space in (pltpu.HBM, pltpu.VMEM))
    operands = (order, base.reshape(steps * fields, rows, LANES), land, tangents, coefficients)
    dma, regular = pltpu.SemaphoreType.DMA, pltpu.SemaphoreType.REGULAR
    return pl.pallas_call(
        functools.partial(steps_kernel, strips, tiles, steps, kept),
        out_shape=(
            jax.ShapeDtypeStruct((modes, 4 * late), jnp.bfloat16),
            jax.ShapeDtypeStruct((fields, modes, rows, LANES), jnp.float32),
            jax.ShapeDtypeStruct((late, fields, rows, LANES), jnp.float32),
        ),
        in_specs=[hbm] * 5,
        out_specs=(vmem, vmem, pl.BlockSpec(memory_space=pl.ANY)),
        scratch_shapes=[
            pltpu.VMEM((everyone, kept, fields, rows, LANES), jnp.float32),
            pltpu.VMEM((tiles, strips, steps * fields + 1, rows, LANES), jnp.float32),
            pltpu.VMEM((kept, strips, fields, rows, columns), jnp.float32),
            pltpu.VMEM((modes, modes), jnp.float32),
            pltpu.VMEM((2 * modes, 2 * modes), jnp.bfloat16),
            pltpu.VMEM((kept, everyone, fields, rows, LANES), jnp.float32),
            pltpu.VMEM((steps, COEFS, tiles, SUB * strips, LANES), jnp.float32),
            pltpu.VMEM((tiles, SUB * strips, LANES), jnp.float32),
            pltpu.VMEM((3, tiles, tall, LANES), jnp.float32),
            pltpu.VMEM((3, tiles, tall, LANES), jnp.float32),
            pltpu.VMEM((tiles, tall, LANES), jnp.float32),
            pltpu.VMEM((2, tiles, tall, LANES), jnp.float32),
            dma((2, strips)), dma((strips,)), dma, dma((tiles,)), dma, dma,
            dma, dma((kept,)), dma, dma, dma,
            regular, regular, regular, regular,
            pltpu.VMEM((rows, LANES), jnp.int32), pltpu.SMEM((steps,), jnp.int32), dma((4,)),
        ],
        compiler_params=pltpu.CompilerParams(
            collective_id=0, has_side_effects=True, vmem_limit_bytes=32 << 20
        ),
    )(*(pltpu.with_memory_space_constraint(held_in_hbm, pltpu.HBM) for held_in_hbm in operands))


def add_last(few_ref, partial_ref, late_ref, out_ref, staged, sems):
    late, spots, _ = late_ref.shape
    groups, modes = partial_ref.shape[:2]
    cells = late_ref.reshape(late * spots, LANES)
    few = few_ref[...]
    copies = []
    for group in range(groups):
        start = partial_ref.at[group].reshape(modes * SUB, LANES)
        out = staged.at[group].reshape(modes * SUB, LANES)
        for spot in range(0, SUB, 2):
            first = SUB * group + spot
            high, low = halves(jnp.concatenate(
                [cells[pl.ds(first + i, late, stride=spots), :] for i in (0, 1)], 1
            ))
            mixed = jnp.dot(
                few, jnp.concatenate([high, low, high, low], 0), preferred_element_type=jnp.float32
            )
            for i in (0, 1):
                row = pl.ds(spot + i, modes, stride=SUB)
                out[row, :] = start[row, :] + mixed[:, LANES * i:LANES * (i + 1)]
        copies.append(pltpu.make_async_copy(
            staged.at[group], out_ref.at[:, pl.ds(SUB * group, SUB)], sems.at[group]
        ))
        copies[-1].start()
    for copy in copies:
        copy.wait()


def mix(few, partial, late):
    groups, modes = partial.shape[:2]
    return pl.pallas_call(
        add_last,
        out_shape=jax.ShapeDtypeStruct((modes, groups * SUB, LANES), jnp.float32),
        in_specs=[pl.BlockSpec(memory_space=pltpu.VMEM)] * 3,
        out_specs=pl.BlockSpec(memory_space=pltpu.HBM),
        scratch_shapes=[
            pltpu.VMEM((groups, modes, SUB, LANES), jnp.float32),
            pltpu.SemaphoreType.DMA((groups,)),
        ],
        compiler_params=pltpu.CompilerParams(vmem_limit_bytes=8 << 20),
    )(few, partial, late)


def on_device_whole(tangents, checkpoints, owner_order, land_mask, coefficients):
    fields, rows = tangents.shape[1:3]
    few, partial, late = step_modes(owner_order, checkpoints, land_mask, tangents, coefficients)
    whole = mix(few, partial, late.reshape(-1, fields * rows, LANES))
    return whole.reshape(-1, fields, rows, LANES)


def on_device(tangents, checkpoints, owner_order, land_mask, coefficients):
    strips = lax.axis_size("rows")
    held, _, rows, columns = tangents.shape
    fits = (
        held % strips == 0 and strips % 2 == 0 and lax.axis_size("mode") % 2 == 0
        and lax.axis_size("mode") > 2 and rows == SUB and checkpoints.shape[-1] == LANES and strips <= 8
        and coefficients.shape[0] == held * lax.axis_size("mode")
        and coefficients.shape[0] % LANES == 0
    )
    chosen = on_device_whole if fits else on_device_general
    return chosen(tangents, checkpoints, owner_order, land_mask, coefficients)


def solution(mesh):
    placed = (
        P("mode", None, "rows", None),
        P(None, None, "rows", "mode"),
        P(),
        P("rows", None),
        P(),
    )
    return jax.shard_map(
        on_device,
        mesh=mesh,
        in_specs=placed,
        out_specs=P(None, None, "rows", "mode"),
        check_vma=False,
    )
```
